256 devices in a mesh: seq: 16 (over x, y), head: 16 (over z, core).
Axes of the slice: x: 4, y: 4, z: 8, core: 2. Of those that a mesh axis runs over, the one named last changes fastest.
Arguments:
- x_heads: bfloat16 [2, 4096, 16384], P(None, 'seq', 'head'), may hold values from -6 to 6
- gate_z: bfloat16 [2, 4096, 16384], P(None, 'seq', 'head'), may hold values from -6 to 6
- b_proj: bfloat16 [2, 4096, 128], P(None, 'seq'), may hold values from -0.59765625 to 0.59765625
- c_proj: bfloat16 [2, 4096, 128], P(None, 'seq'), may hold values from -6 to 6
- dt_raw: float32 [2, 4096, 256], P(None, 'seq', 'head'), may hold values from -3 to 3
- dt_bias: float32 [2, 256], P(None, 'head'), may hold values from -1 to 0.5
- decay_rate: float32 [2, 256], P(None, 'head'), may hold values from 0 to 1, as said below
- skip_d: float32 [2, 256], P(None, 'head'), may hold values from 0.5 to 1.5
- norm_gain: float32 [2, 16384], P(None, 'head'), may hold values from 0.5 to 1.5
- w_out: bfloat16 [2, 16384, 8192], P(None, 'head', 'seq'), may hold values from -0.046875 to 0.046875
- seg_ids: int32 [4096], P('seq'), may hold values from 0 to 8, never falling along the last dimension, each value on 1 to 1024 neighbouring positions
Outputs:
- mixed: bfloat16 [2, 4096, 8192], P(None, 'head', 'seq')
The draws below stay inside these ranges and needn't reach their ends.
Inputs may be any that keep to these rules, and one draw needn't show every extreme that they name: `decay_rate`: Positive. `seg_ids`: document numbers start at 0, never fall along the sequence and take every value; one document has exactly 1024 tokens.
All inputs are finite; a program needn't handle non-finite values.
Results may differ from the reference program's by a relative error of at most 0.019.
Values may be sent and summed in bfloat16 or wider, within the bound.
A program may use at most 128 MiB of HBM per device.

```python
import math
import jax
import jax.numpy as jnp
import numpy as np
from jax import lax

D = 8192
HEADS = 256
HEADDIM = 64
STATE = 128
SPAN = 256
TOKENS = 4096
SEGS = 9
MOST = 1024
N_HEAD = 16


def draw_decay_rate(key, part):
    key_pick, key_slow, key_fast = jax.random.split(key, 3)
    portion = 0.5
    chosen = jax.random.uniform(key_pick, (2, HEADS)) < portion
    slow_log = jax.random.uniform(key_slow, (2, HEADS), minval=jnp.log(0.1 / TOKENS), maxval=jnp.log(1.0 / TOKENS))
    fast_log = jax.random.uniform(key_fast, (2, HEADS), minval=jnp.log(1.0 / 50.0), maxval=jnp.log(1.0 / 30.0))
    return jnp.exp(jnp.where(chosen, slow_log, fast_log)).astype(jnp.float32)


def levels(own_key, shape, cuts, least, largest):
    def one(dim, parts):
        heights = jax.random.uniform(jax.random.fold_in(jax.random.fold_in(own_key, 6), dim), (parts,), jnp.float32, least / len(cuts), largest / len(cuts))
        return jnp.repeat(jnp.exp(heights), shape[dim] // parts).reshape((-1,) + (1,) * (len(shape) - dim - 1))

    factor_of = one(*cuts[0])
    for cut in cuts[1:]:
        factor_of = factor_of * one(*cut)
    return factor_of


def length_profile(amount, total, reach, lean):
    loads = [(1 << 20) // math.isqrt(standing ** lean) + 1 for standing in range(2, amount + 1)]
    spare, counts = total - reach - (amount - 1), [1] * (amount - 1)
    while spare > 0:
        candidates = [i for i in range(amount - 1) if counts[i] < reach]
        whole, remaining = sum([loads[i] for i in candidates]), spare
        for i in candidates:
            more = min(reach - counts[i], max(1, remaining * loads[i] // whole), spare)
            counts[i] = counts[i] + more
            spare = spare - more
    return np.array([reach] + counts)


def ragged_sizes(stream_key, number_of, total, bound, slope):
    if number_of == 2:
        one = jax.random.randint(stream_key, (), max(1, total - bound), min(bound, total - 1) + 1)
        return jnp.stack([one, total - one])
    sizes = jnp.asarray(length_profile(number_of, total, bound, slope), jnp.int32)
    pairs = (number_of - 1) // 2
    donor, receiver = sizes[1:1 + 2 * pairs:2], sizes[2:2 + 2 * pairs:2]
    slack = jnp.minimum(donor - 1, bound - receiver)
    passed = jax.random.randint(jax.random.fold_in(stream_key, 1), (pairs,), 0, 1 << 20) % (slack + 1)
    sizes = sizes.at[1:1 + 2 * pairs:2].set(donor - passed).at[2:2 + 2 * pairs:2].set(receiver + passed)
    return sizes[jax.random.permutation(jax.random.fold_in(stream_key, 2), number_of)]


def noise(rng, extent, scale, limit, cuts=(), held_as=jnp.bfloat16):
    array = jax.random.normal(rng, extent, jnp.float32) * scale
    if len(cuts) > 0:
        array = levels(rng, extent, cuts, -0.22, 0.18) * array
    return jnp.clip(array, min=-limit, max=limit).astype(held_as)


def setup_inputs(seed: int = 0) -> dict:
    seeds = jax.random.split(jax.random.key(seed), 12)
    return {
        "x_heads": noise(seeds[0], (2, TOKENS, HEADS * HEADDIM), 1.0, 6.0, ((1, 16), (2, 16))),
        "gate_z": noise(seeds[1], (2, TOKENS, HEADS * HEADDIM), 1.0, 6.0, ((1, 16), (2, 16))),
        "b_proj": noise(seeds[2], (2, TOKENS, STATE), 0.1, 0.59765625, ((1, 16),)),
        "c_proj": noise(seeds[3], (2, TOKENS, STATE), 1.0, 6.0, ((1, 16),)),
        "dt_raw": noise(seeds[4], (2, TOKENS, HEADS), 0.5, 3.0, ((1, 16), (2, 16)), jnp.float32),
        "dt_bias": jnp.clip(-1.0 + 1.5 * jax.random.uniform(seeds[5], (2, HEADS), jnp.float32) ** levels(seeds[5], (2, HEADS), ((1, 16),), -0.2, 0.2), -1.0, 0.5),
        "decay_rate": draw_decay_rate(jax.random.fold_in(seeds[11], 71), 0),
        "skip_d": jnp.clip(0.5 + 1.0 * jax.random.uniform(seeds[7], (2, HEADS), jnp.float32) ** levels(seeds[7], (2, HEADS), ((1, 16),), -0.2, 0.2), 0.5, 1.5),
        "norm_gain": jnp.clip(0.5 + 1.0 * jax.random.uniform(seeds[8], (2, HEADS * HEADDIM), jnp.float32) ** levels(seeds[8], (2, HEADS * HEADDIM), ((1, 16),), -0.2, 0.2), 0.5, 1.5),
        "w_out": noise(seeds[9], (2, HEADS * HEADDIM, D), (HEADS * HEADDIM) ** -0.5, 0.046875, ((1, 16), (2, 16))),
        "seg_ids": jnp.searchsorted(jnp.cumsum(ragged_sizes(seeds[10], SEGS, TOKENS, MOST, 0)), jnp.arange(TOKENS), side="right").astype(jnp.int32),
    }


highest = lax.Precision.HIGHEST

def to_blocks(tensor, nblocks):
    shaped = tensor.reshape((tensor.shape[0], nblocks, tensor.shape[1] // nblocks) + tensor.shape[2:])
    return jnp.moveaxis(shaped, 1, 0)

def from_blocks(tensor):
    moved = jnp.moveaxis(tensor, 0, 1)
    return moved.reshape((moved.shape[0], moved.shape[1] * moved.shape[2]) + moved.shape[3:])

def span_state(carried, before, offset, anchor, pieces):
    x_block, b_block, c_block, step_block, decay_block, seg_block = pieces
    running = jnp.cumsum(decay_block, axis=1)
    total = running[:, -1, :]
    kept = (seg_block == before).astype(jnp.float32)
    same_last = (seg_block == seg_block[-1]).astype(jnp.float32)
    tail_w = jnp.exp(total[:, None, :] - running) * same_last[None, :, None] * step_block
    fresh = jnp.einsum('mjh,mjhp,mjn->mhpn', tail_w, x_block, b_block, precision=highest)
    new_state = (jnp.exp(total) * kept[-1])[:, :, None, None] * carried + fresh
    factor = jnp.exp(offset[:, None, :] + running) * (seg_block == anchor).astype(jnp.float32)[None, :, None]
    return (new_state, factor, total)

def span_output(carried, before, pieces):
    x_block, b_block, c_block, step_block, decay_block, seg_block = pieces
    running = jnp.cumsum(decay_block, axis=1)
    kept = (seg_block == before).astype(jnp.float32)
    entry_w = jnp.exp(running) * kept[None, :, None]
    places = jnp.arange(seg_block.shape[0], dtype=jnp.int32)
    lower_mask = (places[:, None] >= places[None, :]) & (seg_block[:, None] == seg_block[None, :])
    run_t = jnp.transpose(running, (0, 2, 1))
    spread = run_t[:, :, :, None] - run_t[:, :, None, :]
    mixing = jnp.exp(jnp.minimum(spread, 0.0)) * lower_mask.astype(jnp.float32)
    products = jnp.einsum('min,mjn->mij', c_block, b_block, precision=highest)
    weights = mixing * products[:, None] * jnp.transpose(step_block, (0, 2, 1))[:, :, None, :]
    inside = jnp.einsum('mhij,mjhp->mihp', weights, x_block, precision=highest)
    entering = jnp.einsum('min,mhpn->mihp', c_block, carried, precision=highest)
    return inside + entry_w[..., None] * entering

def scan_turn(carry, pieces):
    carried, before = carry
    output = span_output(carried, before, pieces)
    new_state, factor_unused, total_unused = span_state(carried, before, jnp.zeros(carried.shape[:2], jnp.float32), before, pieces)
    return ((new_state, pieces[5][-1]), output)

def reference(x_heads, gate_z, b_proj, c_proj, dt_raw, dt_bias, decay_rate, skip_d, norm_gain, w_out, seg_ids):
    length = TOKENS
    block = min(SPAN, length)
    nblocks = length // block
    step_size = jax.nn.softplus(dt_raw + dt_bias[:, None, :])
    log_decay = -decay_rate[:, None, :] * step_size
    x_float = x_heads.astype(jnp.float32).reshape(2, length, HEADS, HEADDIM)
    b_float = b_proj.astype(jnp.float32)
    c_float = c_proj.astype(jnp.float32)
    pieces = (to_blocks(x_float, nblocks), to_blocks(b_float, nblocks), to_blocks(c_float, nblocks), to_blocks(step_size, nblocks), to_blocks(log_decay, nblocks), seg_ids.reshape(nblocks, block))
    start = (jnp.zeros((2, HEADS, HEADDIM, STATE), jnp.float32), seg_ids[0])
    end_unused, outputs = lax.scan(scan_turn, start, pieces)
    ssd_out = from_blocks(outputs) + skip_d[:, None, :, None] * x_float
    gated = ssd_out.reshape(2, length, HEADS * HEADDIM) * jax.nn.silu(gate_z.astype(jnp.float32))
    mean_square = lax.optimization_barrier(jnp.mean(gated * gated, axis=2))
    normed = (gated * lax.rsqrt(mean_square + 1e-05)[:, :, None] * norm_gain[:, None, :]).astype(jnp.bfloat16)
    width = HEADS * HEADDIM // N_HEAD
    grouped = normed.reshape(2, length, N_HEAD, width)
    weights = w_out.reshape(2, N_HEAD, width, D)

    def add_group(summed, index):
        part_in = lax.dynamic_index_in_dim(grouped, index, 2, keepdims=False)
        weight_in = lax.dynamic_index_in_dim(weights, index, 1, keepdims=False)
        term = jnp.einsum('mtk,mkd->mtd', part_in.astype(jnp.float32), weight_in.astype(jnp.float32))
        rounded = lax.optimization_barrier(term.astype(jnp.bfloat16))
        return (summed + rounded.astype(jnp.float32), None)
    summed, unused = lax.scan(add_group, jnp.zeros((2, length, D), jnp.float32), jnp.arange(N_HEAD, dtype=jnp.int32))
    return summed.astype(jnp.bfloat16)
```

```python
import jax
import jax.numpy as jnp
from jax import lax
from jax.sharding import PartitionSpec as P

HEADS = 256
HEADDIM = 64
SPAN = 256


highest = lax.Precision.HIGHEST


def passed_along(block, axis, distance):
    devices = range(lax.axis_size(axis))
    route = [(i - distance, i) for i in devices if i - distance in devices]
    return lax.ppermute(block, axis, route)


def to_blocks(tensor, nblocks):
    shaped = tensor.reshape(
        (tensor.shape[0], nblocks, tensor.shape[1] // nblocks) + tensor.shape[2:]
    )
    return jnp.moveaxis(shaped, 1, 0)


def from_blocks(tensor):
    moved = jnp.moveaxis(tensor, 0, 1)
    return moved.reshape((moved.shape[0], moved.shape[1] * moved.shape[2]) + moved.shape[3:])


def span_state(carried, before, offset, anchor, pieces):
    x_block, b_block, c_block, step_block, decay_block, seg_block = pieces
    running = jnp.cumsum(decay_block, axis=1)
    total = running[:, -1, :]
    kept = (seg_block == before).astype(jnp.float32)
    same_last = (seg_block == seg_block[-1]).astype(jnp.float32)
    tail_w = jnp.exp(total[:, None, :] - running) * same_last[None, :, None] * step_block
    fresh = jnp.einsum("mjh,mjhp,mjn->mhpn", tail_w, x_block, b_block, precision=highest)
    new_state = (jnp.exp(total) * kept[-1])[:, :, None, None] * carried + fresh
    factor = (
        jnp.exp(offset[:, None, :] + running)
        * (seg_block == anchor).astype(jnp.float32)[None, :, None]
    )
    return (new_state, factor, total)


def span_output(carried, before, pieces):
    x_block, b_block, c_block, step_block, decay_block, seg_block = pieces
    running = jnp.cumsum(decay_block, axis=1)
    kept = (seg_block == before).astype(jnp.float32)
    entry_w = jnp.exp(running) * kept[None, :, None]
    places = jnp.arange(seg_block.shape[0], dtype=jnp.int32)
    lower_mask = (places[:, None] >= places[None, :]) & (seg_block[:, None] == seg_block[None, :])
    run_t = jnp.transpose(running, (0, 2, 1))
    spread = run_t[:, :, :, None] - run_t[:, :, None, :]
    mixing = jnp.exp(jnp.minimum(spread, 0.0)) * lower_mask.astype(jnp.float32)
    products = jnp.einsum("min,mjn->mij", c_block, b_block, precision=highest)
    weights = mixing * products[:, None] * jnp.transpose(step_block, (0, 2, 1))[:, :, None, :]
    inside = jnp.einsum("mhij,mjhp->mihp", weights, x_block, precision=highest)
    entering = jnp.einsum("min,mhpn->mihp", c_block, carried, precision=highest)
    return inside + entry_w[..., None] * entering


def local(
    x_heads, gate_z, b_proj, c_proj, dt_raw, dt_bias, decay_rate, skip_d, norm_gain, w_out, seg_ids
):
    rows = x_heads.shape[1]
    local_heads = dt_raw.shape[2]
    head_size = x_heads.shape[2] // local_heads
    block = min(SPAN, rows)
    nblocks = rows // block
    step_size = jax.nn.softplus(dt_raw + dt_bias[:, None, :])
    log_decay = -decay_rate[:, None, :] * step_size
    x_float = x_heads.astype(jnp.float32).reshape(2, rows, local_heads, head_size)
    b_float = b_proj.astype(jnp.float32)
    c_float = c_proj.astype(jnp.float32)
    pieces = (
        to_blocks(x_float, nblocks),
        to_blocks(b_float, nblocks),
        to_blocks(c_float, nblocks),
        to_blocks(step_size, nblocks),
        to_blocks(log_decay, nblocks),
        seg_ids.reshape(nblocks, block),
    )
    anchor = passed_along(seg_ids[rows - 1 :], "seq", 1)[0]
    offset_zero = jnp.zeros((2, local_heads), jnp.float32)
    empty = jnp.zeros((2, local_heads, head_size, b_proj.shape[2]), jnp.float32)

    def joint_turn(carry, piece_set):
        carried, before, offset = carry
        output = span_output(carried, before, piece_set)
        new_state, factor, total = span_state(carried, before, offset, anchor, piece_set)
        return ((new_state, piece_set[5][-1], offset + total), (output, factor))

    ends, (outputs, factors) = lax.scan(joint_turn, (empty, anchor, offset_zero), pieces)
    local_state = ends[0]
    factor_all = from_blocks(factors)
    decay_dev = factor_all[:, -1, :]

    decay_one = passed_along(decay_dev, "seq", 1)
    decay_two = passed_along(decay_dev, "seq", 2)
    earlier = passed_along(local_state.astype(jnp.bfloat16), "seq", 1).astype(jnp.float32)
    pair_state = (local_state + decay_dev[:, :, None, None] * earlier).astype(jnp.bfloat16)
    near = passed_along(pair_state, "seq", 1).astype(jnp.float32)
    far = passed_along(pair_state, "seq", 3).astype(jnp.float32)
    state_in = near + (decay_one * decay_two)[:, :, None, None] * far
    entering = jnp.einsum("mtn,mhpn->mthp", c_float, state_in, precision=highest)
    ssd_out = (
        from_blocks(outputs) + factor_all[..., None] * entering + skip_d[:, None, :, None] * x_float
    )
    gated = ssd_out.reshape(2, rows, local_heads * head_size) * jax.nn.silu(
        gate_z.astype(jnp.float32)
    )
    square_sum = lax.psum(jnp.sum(gated * gated, axis=2), "head")
    mean_square = square_sum / (HEADS * HEADDIM)
    normed = (gated * lax.rsqrt(mean_square + 1e-05)[:, :, None] * norm_gain[:, None, :]).astype(
        jnp.bfloat16
    )
    partial_terms = jnp.einsum(
        "mtk,mkd->mtd",
        lax.all_gather(normed, "seq", axis=1, tiled=True),
        w_out,
        preferred_element_type=jnp.float32,
    )
    summed = lax.psum_scatter(
        partial_terms.astype(jnp.bfloat16), "head", scatter_dimension=1, tiled=True
    )
    return summed


def solution(mesh):
    placed = (
        P(None, "seq", "head"),
        P(None, "seq", "head"),
        P(None, "seq", None),
        P(None, "seq", None),
        P(None, "seq", "head"),
        P(None, "head"),
        P(None, "head"),
        P(None, "head"),
        P(None, "head"),
        P(None, "head", "seq"),
        P("seq"),
    )
    return jax.shard_map(
        local, mesh=mesh, in_specs=placed, out_specs=P(None, "head", "seq"), check_vma=False
    )
```

```python
import jax
import jax.numpy as jnp
from jax import lax
from jax.experimental import pallas as pl
from jax.experimental.pallas import tpu as pltpu
from jax.sharding import PartitionSpec as P

HEADS = 256
HEADDIM = 64
SPAN = 256


highest = lax.Precision.HIGHEST


def passed_along(block, axis, distance):
    devices = range(lax.axis_size(axis))
    route = [(i - distance, i) for i in devices if i - distance in devices]
    return lax.ppermute(block, axis, route)


def to_blocks(tensor, nblocks):
    shaped = tensor.reshape(
        (tensor.shape[0], nblocks, tensor.shape[1] // nblocks) + tensor.shape[2:]
    )
    return jnp.moveaxis(shaped, 1, 0)


def from_blocks(tensor):
    moved = jnp.moveaxis(tensor, 0, 1)
    return moved.reshape((moved.shape[0], moved.shape[1] * moved.shape[2]) + moved.shape[3:])


def span_state(carried, before, offset, anchor, pieces):
    x_block, b_block, c_block, step_block, decay_block, seg_block = pieces
    running = jnp.cumsum(decay_block, axis=1)
    total = running[:, -1, :]
    kept = (seg_block == before).astype(jnp.float32)
    same_last = (seg_block == seg_block[-1]).astype(jnp.float32)
    tail_w = jnp.exp(total[:, None, :] - running) * same_last[None, :, None] * step_block
    fresh = jnp.einsum("mjh,mjhp,mjn->mhpn", tail_w, x_block, b_block, precision=highest)
    new_state = (jnp.exp(total) * kept[-1])[:, :, None, None] * carried + fresh
    factor = (
        jnp.exp(offset[:, None, :] + running)
        * (seg_block == anchor).astype(jnp.float32)[None, :, None]
    )
    return (new_state, factor, total)


def span_output(carried, before, pieces):
    x_block, b_block, c_block, step_block, decay_block, seg_block = pieces
    running = jnp.cumsum(decay_block, axis=1)
    kept = (seg_block == before).astype(jnp.float32)
    entry_w = jnp.exp(running) * kept[None, :, None]
    places = jnp.arange(seg_block.shape[0], dtype=jnp.int32)
    lower_mask = (places[:, None] >= places[None, :]) & (seg_block[:, None] == seg_block[None, :])
    run_t = jnp.transpose(running, (0, 2, 1))
    spread = run_t[:, :, :, None] - run_t[:, :, None, :]
    mixing = jnp.exp(jnp.minimum(spread, 0.0)) * lower_mask.astype(jnp.float32)
    products = jnp.einsum("min,mjn->mij", c_block, b_block, precision=highest)
    weights = mixing * products[:, None] * jnp.transpose(step_block, (0, 2, 1))[:, :, None, :]
    inside = jnp.einsum("mhij,mjhp->mihp", weights, x_block, precision=highest)
    entering = jnp.einsum("min,mhpn->mihp", c_block, carried, precision=highest)
    return inside + entry_w[..., None] * entering


MESH = pl.DeviceIdType.MESH
XS, YS, ZS = 4, 4, 8


class Copies:
    def __init__(self, send, recv):
        self.send, self.recv, self.used = send, recv, 0

    def take(self, count=1):
        first = self.used
        self.used += count
        return first

    def remote(self, src, dst, slot, device):
        return pltpu.make_async_remote_copy(
            src_ref=src,
            dst_ref=dst,
            send_sem=self.send.at[slot],
            recv_sem=self.recv.at[slot],
            device_id=device,
            device_id_type=MESH,
        )


def tail_kernel(n_ref, ss_ref, w_ref, out_ref, wf, nf, part, ring, fin_src, fin, sums, send, recv, local):
    seq, head = lax.axis_index("seq"), lax.axis_index("head")
    x, y = seq // YS, seq % YS
    z, c = head // 2, head % 2
    other = 1 - c

    def device(x_at, y_at, z_at, c_at):
        return {"seq": x_at * YS + y_at, "head": z_at * 2 + c_at}

    copies = Copies(send, recv)
    started = []

    def start(copy):
        copy.start()
        started.append(copy)
        return copy

    sibling = device(x, y, z, other)

    def weight_at(model):
        return y if model == 0 else x

    def weight_peer(model, step):
        if model == 0:
            return device(x, (y + step) % YS, z, c)
        return device((x + step) % XS, y, z, c)

    def token_at(model):
        return x if model == 0 else y

    def token_peer(model, step, core):
        if model == 0:
            return device((x + step) % XS, y, z, core)
        return device(x, (y + step) % YS, z, core)

    half = wf.shape[3] // 2
    rows = nf.shape[3]
    top, bottom = pl.ds(0, half), pl.ds(half, half)
    weights_in = []
    forward_later = []
    own_local = []
    for model in (0, 1):
        at = weight_at(model)
        own = pltpu.make_async_copy(w_ref.at[model], wf.at[model, at, c], local.at[model])
        own.start()
        own_local.append(own)
        first = copies.take(4)
        order = ((1, top, 0), (-1, bottom, 1), (1, bottom, 2), (-1, top, 3))
        for step, part_rows, n in order:
            copy = start(
                copies.remote(
                    w_ref.at[model, part_rows],
                    wf.at[model, at, c, part_rows],
                    first + n,
                    weight_peer(model, step),
                )
            )
            weights_in.append((model, step, part_rows, n, copy))
        slot = copies.take()
        to_sibling = start(
            copies.remote(w_ref.at[model], wf.at[model, at, c], slot, sibling)
        )
        forward_later.append(to_sibling)

    sums_first = copies.take(16)
    sums_local = pltpu.make_async_copy(ss_ref, sums.at[head], local.at[2])
    sums_sent = []
    for i in range(16):
        copy = pltpu.make_async_remote_copy(
            src_ref=ss_ref,
            dst_ref=sums.at[head],
            send_sem=send.at[sums_first + i],
            recv_sem=recv.at[sums_first + head],
            device_id={"seq": (seq + i) % 16, "head": seq},
            device_id_type=MESH,
        )
        sums_sent.append(copy)
        if i == 0:
            pl.when(head != seq)(copy.start)
            pl.when(head == seq)(sums_local.start)
        else:
            copy.start()

    token_in = {}
    token_own = []
    for model in (0, 1):
        at = token_at(model)
        mine = pl.ds(pl.multiple_of(c * rows, rows), rows)
        theirs = pl.ds(pl.multiple_of(other * rows, rows), rows)
        own = pltpu.make_async_copy(n_ref.at[model, mine], nf.at[model, c, at], local.at[3 + model])
        own.start()
        token_own.append(own)
        first = copies.take(8)
        to_sibling = start(
            copies.remote(n_ref.at[model, theirs], nf.at[model, c, at], first + 4, sibling)
        )
        sends = []
        for core in (0, 1):
            for n, step in ((0, 1), (1, -1)):
                piece = n_ref.at[model, pl.ds(core * rows, rows)]
                copy = pltpu.make_async_remote_copy(
                    src_ref=piece,
                    dst_ref=nf.at[model, c, at],
                    send_sem=send.at[first + 2 * core + n],
                    recv_sem=recv.at[first + 2 * c + n],
                    device_id=token_peer(model, step, core),
                    device_id_type=MESH,
                )
                sends.append(start(copy))
        token_in[model] = (first, to_sibling)

    def arrival(dst, slot):
        return copies.remote(dst, dst, slot, sibling)

    size = YS
    sibling_waits = []
    opposite = []
    for model in (0, 1):
        at = weight_at(model)
        for step, part_rows, n, copy in [w[1:] for w in weights_in if w[0] == model]:
            source = (at - step + size) % size
            copy.wait_recv()
            if n < 2:
                slot = copies.take()
                onward = start(
                    copies.remote(
                        wf.at[model, source, c, part_rows],
                        wf.at[model, source, c, part_rows],
                        slot,
                        weight_peer(model, step),
                    )
                )
                opposite.append((model, step, part_rows, onward))
            slot = copies.take()
            sibling_waits.append(
                start(
                    copies.remote(
                        wf.at[model, source, c, part_rows],
                        wf.at[model, source, c, part_rows],
                        slot,
                        sibling,
                    )
                )
            )
    for model, step, part_rows, onward in opposite:
        at = weight_at(model)
        source = (at - 2 * step + 2 * size) % size
        onward.wait_recv()
        slot = copies.take()
        sibling_waits.append(
            start(
                copies.remote(
                    wf.at[model, source, c, part_rows],
                    wf.at[model, source, c, part_rows],
                    slot,
                    sibling,
                )
            )
        )

    token_forward = {}
    for model in (0, 1):
        at = token_at(model)
        first, to_sibling = token_in[model]
        forwards = []
        for core, n, step in ((0, 0, 1), (1, 1, -1), (1, 0, 1), (0, 1, -1)):
            source = (at - step + size) % size
            arrival(nf.at[model, core, source], first + 2 * core + n).wait_recv()
            if core == n:
                forwards.append(
                    start(
                        copies.remote(
                            nf.at[model, core, source],
                            nf.at[model, core, source],
                            first + 5 + n,
                            token_peer(model, step, c),
                        )
                    )
                )
        token_forward[model] = (to_sibling, forwards)

    for own in own_local:
        own.wait()
    for copy in forward_later + sibling_waits:
        copy.wait_recv()

    def piece(model, z_to, e):
        if model == 0:
            return part.at[0, z_to // 2, 2 * (z_to % 2) + e]
        return part.at[1, 2 * (z_to % 2) + e, z_to // 2]

    ring_first = copies.take(28)
    sent_ring = {}

    def ring_step(model, k):
        for e, step in ((0, 1), (1, -1)):
            z_to = (z - step * (1 + k) + 2 * ZS) % ZS
            if k == 0:
                src = piece(model, z_to, e)
            else:
                sent_ring[model, e, k - 1].wait_recv()
                src = ring.at[model, e, k - 1]
                src[...] = (
                    src[...].astype(jnp.float32) + piece(model, z_to, e)[...].astype(jnp.float32)
                ).astype(src.dtype)
            copy = start(
                copies.remote(
                    src,
                    ring.at[model, e, k],
                    ring_first + 14 * model + 7 * e + k,
                    device(x, y, (z + step + ZS) % ZS, c),
                )
            )
            sent_ring[model, e, k] = copy

    def multiply(model, j):
        total = None
        for core in (0, 1):
            tokens = nf[model, core].reshape(4 * rows, nf.shape[4])
            term = jnp.dot(tokens, wf[model, j, core], preferred_element_type=jnp.float32)
            total = term if total is None else total + term
        part[model, :, j] = total.reshape(4, rows, total.shape[1]).astype(part.dtype)

    fin_first = copies.take(8)
    finals = []

    def finish(model):
        for e in (0, 1):
            sent_ring[model, e, 6].wait_recv()
            fin_src[model, e] = (
                ring[model, e, 6].astype(jnp.float32)
                + piece(model, z, e)[...].astype(jnp.float32)
            ).astype(fin_src.dtype)
            if model == 0:
                target = device(x, 2 * (z % 2) + e, 2 * (z // 2) + y // 2, y % 2)
                is_self = jnp.logical_and(
                    jnp.logical_and(z % 2 == y // 2, c == y % 2), y % 2 == e
                )
            else:
                target = device(z // 2, y, 2 * x + z % 2, e)
                is_self = jnp.logical_and(z // 2 == x, c == e)
            copy = pltpu.make_async_remote_copy(
                src_ref=fin_src.at[model, e],
                dst_ref=fin.at[model, c],
                send_sem=send.at[fin_first + 4 * model + e],
                recv_sem=recv.at[fin_first + 4 * model + c],
                device_id=target,
                device_id_type=MESH,
            )
            here = pltpu.make_async_copy(
                fin_src.at[model, e], fin.at[model, c], local.at[5 + 2 * model + e]
            )
            pl.when(jnp.logical_not(is_self))(copy.start)
            pl.when(is_self)(here.start)
            finals.append((is_self, copy, here))

    for model in (0, 1):
        first, to_sibling = token_in[model]
        to_sibling, forwards = token_forward[model]
        token_own[model].wait()
        to_sibling.wait_recv()
        for copy in forwards:
            copy.wait_recv()
        for j in range(4):
            multiply(model, j)
            if model == 1 and j % 2 == 1:
                ring_step(0, (j + 1) // 2)
        ring_step(model, 0)

    for k in range(3, 7):
        ring_step(0, k)
        ring_step(1, k - 2)
    finish(0)
    ring_step(1, 5)
    ring_step(1, 6)

    for i in range(16):
        here = jnp.logical_and(seq == head, head == i)
        arrived = pltpu.make_async_remote_copy(
            src_ref=ss_ref,
            dst_ref=sums.at[i],
            send_sem=send.at[sums_first + i],
            recv_sem=recv.at[sums_first + i],
            device_id=sibling,
            device_id_type=MESH,
        )
        pl.when(here)(sums_local.wait)
        pl.when(jnp.logical_not(here))(arrived.wait_recv)
    mean_square = jnp.sum(sums[...], axis=0) / 16384.0
    scale = lax.rsqrt(mean_square + 1e-05)
    columns = jnp.concatenate([scale] * 16, axis=0).T

    finish(1)
    for model in (0, 1):
        for core in (0, 1):
            if model == 0:
                from_self = jnp.logical_and(
                    jnp.logical_and(z % 2 == y // 2, c == y % 2), c == core
                )
                e = y % 2
            else:
                from_self = jnp.logical_and(z // 2 == x, c == core)
                e = c
            arrived = copies.remote(
                fin_src.at[model, 0], fin.at[model, core], fin_first + 4 * model + core, sibling
            )
            pl.when(jnp.logical_not(from_self))(arrived.wait_recv)

            @pl.when(from_self)
            def _():
                pltpu.make_async_copy(
                    fin_src.at[model, 0], fin.at[model, core], local.at[5 + 2 * model + e]
                ).wait()

            out_ref[model, core * rows : (core + 1) * rows] = (
                fin[model, core].astype(jnp.float32)
                * columns[:, 2 * model + core : 2 * model + core + 1]
            ).astype(out_ref.dtype)

    for copy in started:
        copy.wait_send()
    for i, copy in enumerate(sums_sent):
        if i == 0:
            pl.when(head != seq)(copy.wait_send)
        else:
            copy.wait_send()
    for is_self, copy, here in finals:
        pl.when(jnp.logical_not(is_self))(copy.wait_send)


def tail(normed, squares, w_out):
    depth, width = w_out.shape[1], w_out.shape[2]
    rows = normed.shape[1] // 2
    packed = jnp.pad(squares.reshape(4, 128), ((0, 4), (0, 0)))
    vmem = pl.BlockSpec(memory_space=pltpu.VMEM)
    count = 120
    return pl.pallas_call(
        tail_kernel,
        out_shape=jax.ShapeDtypeStruct((2, 2 * rows, width), jnp.bfloat16),
        in_specs=[vmem, vmem, pl.BlockSpec(memory_space=pl.ANY)],
        out_specs=vmem,
        scratch_shapes=[
            pltpu.VMEM((2, 4, 2, depth, width), jnp.bfloat16),
            pltpu.VMEM((2, 2, 4, rows, depth), jnp.bfloat16),
            pltpu.VMEM((2, 4, 4, rows, width), jnp.bfloat16),
            pltpu.VMEM((2, 2, 7, rows, width), jnp.bfloat16),
            pltpu.VMEM((2, 2, rows, width), jnp.bfloat16),
            pltpu.VMEM((2, 2, rows, width), jnp.bfloat16),
            pltpu.VMEM((16, 8, 128), jnp.float32),
            pltpu.SemaphoreType.DMA((count,)),
            pltpu.SemaphoreType.DMA((count,)),
            pltpu.SemaphoreType.DMA((9,)),
        ],
        compiler_params=pltpu.CompilerParams(
            has_side_effects=True, vmem_limit_bytes=60 * 1024 * 1024
        ),
    )(normed, packed, w_out)


def local(
    x_heads, gate_z, b_proj, c_proj, dt_raw, dt_bias, decay_rate, skip_d, norm_gain, w_out, seg_ids
):
    rows = x_heads.shape[1]
    local_heads = dt_raw.shape[2]
    head_size = x_heads.shape[2] // local_heads
    block = min(SPAN, rows)
    nblocks = rows // block
    step_size = jax.nn.softplus(dt_raw + dt_bias[:, None, :])
    log_decay = -decay_rate[:, None, :] * step_size
    x_float = x_heads.astype(jnp.float32).reshape(2, rows, local_heads, head_size)
    b_float = b_proj.astype(jnp.float32)
    c_float = c_proj.astype(jnp.float32)
    pieces = (
        to_blocks(x_float, nblocks),
        to_blocks(b_float, nblocks),
        to_blocks(c_float, nblocks),
        to_blocks(step_size, nblocks),
        to_blocks(log_decay, nblocks),
        seg_ids.reshape(nblocks, block),
    )
    anchor = passed_along(seg_ids[rows - 1 :], "seq", 1)[0]
    offset_zero = jnp.zeros((2, local_heads), jnp.float32)
    empty = jnp.zeros((2, local_heads, head_size, b_proj.shape[2]), jnp.float32)

    def joint_turn(carry, piece_set):
        carried, before, offset = carry
        output = span_output(carried, before, piece_set)
        new_state, factor, total = span_state(carried, before, offset, anchor, piece_set)
        return ((new_state, piece_set[5][-1], offset + total), (output, factor))

    ends, (outputs, factors) = lax.scan(joint_turn, (empty, anchor, offset_zero), pieces)
    local_state = ends[0]
    factor_all = from_blocks(factors)
    decay_dev = factor_all[:, -1, :]

    decay_one = passed_along(decay_dev, "seq", 1)
    decay_two = passed_along(decay_dev, "seq", 2)
    earlier = passed_along(local_state.astype(jnp.bfloat16), "seq", 1).astype(jnp.float32)
    pair_state = (local_state + decay_dev[:, :, None, None] * earlier).astype(jnp.bfloat16)
    near = passed_along(pair_state, "seq", 1).astype(jnp.float32)
    far = passed_along(pair_state, "seq", 3).astype(jnp.float32)
    state_in = near + (decay_one * decay_two)[:, :, None, None] * far
    entering = jnp.einsum("mtn,mhpn->mthp", c_float, state_in, precision=highest)
    ssd_out = (
        from_blocks(outputs) + factor_all[..., None] * entering + skip_d[:, None, :, None] * x_float
    )
    gated = ssd_out.reshape(2, rows, local_heads * head_size) * jax.nn.silu(
        gate_z.astype(jnp.float32)
    )
    squares = jnp.sum(gated * gated, axis=2)
    raised = (gated * norm_gain[:, None, :]).astype(jnp.bfloat16)
    return tail(raised, squares, w_out)


def solution(mesh):
    placed = (
        P(None, "seq", "head"),
        P(None, "seq", "head"),
        P(None, "seq", None),
        P(None, "seq", None),
        P(None, "seq", "head"),
        P(None, "head"),
        P(None, "head"),
        P(None, "head"),
        P(None, "head"),
        P(None, "head", "seq"),
        P("seq"),
    )
    return jax.shard_map(
        local, mesh=mesh, in_specs=placed, out_specs=P(None, "head", "seq"), check_vma=False
    )
```

```python
import jax
import jax.numpy as jnp
from jax import lax
from jax.experimental import pallas as pl
from jax.experimental.pallas import tpu as pltpu
from jax.sharding import PartitionSpec as P

highest = lax.Precision.HIGHEST
FAR = -1e30

MESH = pl.DeviceIdType.MESH
XS, YS, ZS = 4, 4, 8


class Copies:
    def __init__(self, send, recv):
        self.send, self.recv, self.used = send, recv, 0

    def take(self, count=1):
        first = self.used
        self.used += count
        return first

    def remote(self, src, dst, slot, device):
        return pltpu.make_async_remote_copy(
            src_ref=src,
            dst_ref=dst,
            send_sem=self.send.at[slot],
            recv_sem=self.recv.at[slot],
            device_id=device,
            device_id_type=MESH,
        )


def layer_kernel(
    x_hbm, g_hbm, b_ref, c_ref, dt_ref, bias_ref, rate_ref, skip_ref, gain_ref, seg_ref, w_ref,
    out_ref,
    xv, gv, n_ref, ss_ref, inner, mask, products, spread, seg_own, seg_before,
    local_state, state_out, state_in, pair_out, pair_in, decay_out, decay_in,
    wf, nf, part, ring, fin_src, fin, sums, send, recv, local,
):
    seq, head = lax.axis_index("seq"), lax.axis_index("head")
    x, y = seq // YS, seq % YS
    z, c = head // 2, head % 2
    other = 1 - c

    def device(x_at, y_at, z_at, c_at):
        return {"seq": x_at * YS + y_at, "head": z_at * 2 + c_at}

    copies = Copies(send, recv)
    started = []

    def start(copy):
        copy.start()
        started.append(copy)
        return copy

    sibling = device(x, y, z, other)

    def weight_at(model):
        return y if model == 0 else x

    def weight_peer(model, step):
        if model == 0:
            return device(x, (y + step) % YS, z, c)
        return device((x + step) % XS, y, z, c)

    def token_at(model):
        return x if model == 0 else y

    def token_peer(model, step, core):
        if model == 0:
            return device((x + step) % XS, y, z, core)
        return device(x, (y + step) % YS, z, core)

    half = wf.shape[3] // 2
    rows = nf.shape[3]
    tokens, lanes = xv.shape[1], xv.shape[2]
    heads = dt_ref.shape[2]
    upper, lower = pl.ds(0, half), pl.ds(half, half)

    x_copy = pltpu.make_async_copy(x_hbm, xv, local.at[9])
    g_copy = pltpu.make_async_copy(g_hbm, gv, local.at[10])
    x_copy.start()

    def follower(distance):
        return {"seq": (seq + distance) % 16, "head": head}

    seg_row = seg_ref[...].astype(jnp.float32)
    seg_own[...] = jnp.broadcast_to(seg_row, seg_own.shape)
    seg_copy = start(copies.remote(seg_own, seg_before, copies.take(), follower(1)))

    weights_in = []
    own_local = []
    weight_slot = [copies.take(5) for model in (0, 1)]
    order = ((1, upper, 0), (-1, lower, 1), (1, lower, 2), (-1, upper, 3))

    def send_weights(model, which):
        at = weight_at(model)
        for step, part_rows, n in order:
            if n in which:
                copy = start(
                    copies.remote(
                        w_ref.at[model, part_rows],
                        wf.at[model, at, c, part_rows],
                        weight_slot[model] + n,
                        weight_peer(model, step),
                    )
                )
                weights_in.append((model, step, part_rows, n, copy))

    send_weights(1, (0, 1))
    send_weights(0, (1,))
    send_weights(1, (2, 3))
    send_weights(0, (3,))
    g_copy.start()
    forward_later = []
    for model in (0, 1):
        at = weight_at(model)
        own = pltpu.make_async_copy(w_ref.at[model], wf.at[model, at, c], local.at[model])
        own.start()
        own_local.append(own)
        forward_later.append(
            start(
                copies.remote(
                    w_ref.at[model], wf.at[model, at, c], weight_slot[model] + 4, sibling
                )
            )
        )

    row_at = lax.broadcasted_iota(jnp.int32, (tokens, tokens), 0)
    col_at = lax.broadcasted_iota(jnp.int32, (tokens, tokens), 1)
    eye = (row_at == col_at).astype(jnp.float32)
    lower_ones = (row_at >= col_at).astype(jnp.float32)
    seg_col = lax.dot_general(
        eye, seg_own[...], (((1,), (1,)), ((), ())), precision=highest
    )[:, 0:1]
    mask[...] = jnp.where(
        jnp.logical_and(row_at >= col_at, jnp.abs(seg_col - seg_row) < 0.5), 0.0, FAR
    )
    spread[...] = (
        lax.broadcasted_iota(jnp.int32, spread.shape, 0)
        == lax.broadcasted_iota(jnp.int32, spread.shape, 1) // (lanes // heads)
    ).astype(spread.dtype)
    same_last = (jnp.abs(seg_col - seg_row[:, tokens - 1 : tokens]) < 0.5).astype(jnp.float32)

    def widen(values, columns):
        coarse = values.astype(jnp.bfloat16)
        fine = (values - coarse.astype(jnp.float32)).astype(jnp.bfloat16)
        table = spread[:, columns]
        return jnp.dot(coarse, table, preferred_element_type=jnp.float32) + jnp.dot(
            fine, table, preferred_element_type=jnp.float32
        )

    blocks = [pl.ds(start_at, 256) for start_at in range(0, lanes, 256)]
    state_first = copies.take(2)
    state_copies, running, shifted, totals = [], [], [], []
    x_copy.wait()
    for model in (0, 1):
        raw = dt_ref[model] + bias_ref[model : model + 1, :]
        step_size = jnp.maximum(raw, 0.0) + jnp.log1p(jnp.exp(-jnp.abs(raw)))
        log_decay = -(rate_ref[model : model + 1, :] * step_size)
        run = jnp.dot(lower_ones, log_decay, precision=highest)
        total = run[tokens - 1 : tokens, :]
        tail_w = jnp.exp(total - run) * same_last * step_size
        for block in blocks:
            weighted = (xv[model, :, block].astype(jnp.float32) * widen(tail_w, block)).astype(
                jnp.bfloat16
            )
            fresh = lax.dot_general(
                b_ref[model],
                weighted,
                (((0,), (0,)), ((), ())),
                preferred_element_type=jnp.float32,
            )
            local_state[model, :, block] = fresh
            state_out[model, :, block] = fresh.astype(jnp.bfloat16)
        state_copies.append(
            start(
                copies.remote(
                    state_out.at[model], state_in.at[model], state_first + model, follower(1)
                )
            )
        )
        running.append(run)
        totals.append(total)
        shifted.append(run - jnp.log(step_size))
    send_weights(0, (0,))

    seg_copy.wait_recv()
    anchor = seg_before[0:1, tokens - 1 : tokens]
    has_before = jnp.where(seq > 0, 1.0, 0.0)
    entered = (jnp.abs(seg_col - anchor) < 0.5).astype(jnp.float32) * has_before
    for model in (0, 1):
        kept = jnp.exp(totals[model]) * entered[tokens - 1 : tokens, :]
        kept = jnp.broadcast_to(kept, (8, heads))
        for block in blocks:
            decay_out[model, :, block] = widen(kept, block)
    decay_first = copies.take(2)
    decay_copies = [
        start(copies.remote(decay_out, decay_in.at[i], decay_first + i, follower(i + 1)))
        for i in (0, 1)
    ]

    def inside(model):
        run = running[model]
        shifted_t = lax.dot_general(
            shifted[model], eye, (((0,), (0,)), ((), ())), precision=highest
        )
        products[...] = lax.dot_general(
            c_ref[model],
            b_ref[model],
            (((1,), (1,)), ((), ())),
            preferred_element_type=jnp.float32,
        )
        lane = lax.broadcasted_iota(jnp.int32, (1, 128), 1)
        skip = jnp.broadcast_to(skip_ref[model : model + 1, :], (8, heads))
        mid = tokens // 2
        for pair in range(heads // 2):
            columns = pl.ds(128 * pair, 128)
            x_pair = xv[model, :, columns]
            early = late = None
            for q in (0, 1):
                h = 2 * pair + q
                x_one = x_pair * (lane // 64 == q).astype(jnp.bfloat16)
                gap = run[:mid, h : h + 1] - shifted_t[h : h + 1, :mid] + mask[:mid, :mid]
                weights = (jnp.exp(gap) * products[:mid, :mid]).astype(jnp.bfloat16)
                term = jnp.dot(weights, x_one[:mid], preferred_element_type=jnp.float32)
                early = term if early is None else early + term
                gap = run[mid:, h : h + 1] - shifted_t[h : h + 1, :] + mask[mid:, :]
                weights = (jnp.exp(gap) * products[mid:, :]).astype(jnp.bfloat16)
                term = jnp.dot(weights, x_one, preferred_element_type=jnp.float32)
                late = term if late is None else late + term
            passed = x_pair.astype(jnp.float32) * widen(skip, columns)[0:1, :]
            inner[model, :mid, columns] = early + passed[:mid]
            inner[model, mid:, columns] = late + passed[mid:]

    pair_first = copies.take(4)
    pair_copies = []

    def join_pair(model):
        state_copies[model].wait_recv()
        for block in blocks:
            pair_out[model, :, block] = (
                local_state[model, :, block]
                + decay_out[model, 0:1, block] * state_in[model, :, block].astype(jnp.float32)
            ).astype(jnp.bfloat16)
        pair_copies.append(
            [
                start(
                    copies.remote(
                        pair_out.at[model],
                        pair_in.at[model, i],
                        pair_first + 2 * model + i,
                        follower(1 + 2 * i),
                    )
                )
                for i in (0, 1)
            ]
        )

    def gate(model):
        entry_w = jnp.exp(running[model]) * entered
        squares = jnp.zeros((tokens, 128), jnp.float32)
        for copy in pair_copies[model]:
            copy.wait_recv()
        for block in blocks:
            earlier = pair_in[model, 0, :, block].astype(jnp.float32) + (
                decay_in[0, model, 0:1, block] * decay_in[1, model, 0:1, block]
            ) * pair_in[model, 1, :, block].astype(jnp.float32)
            entering = jnp.dot(
                c_ref[model], earlier.astype(jnp.bfloat16), preferred_element_type=jnp.float32
            )
            ssd_out = inner[model, :, block] + widen(entry_w, block) * entering
            opened = gv[model, :, block].astype(jnp.float32)
            gated = ssd_out * (opened / (1.0 + jnp.exp(-opened)))
            squares = squares + (
                gated[:, :128] * gated[:, :128] + gated[:, 128:] * gated[:, 128:]
            )
            n_ref[model, :, block] = (gated * gain_ref[model : model + 1, block]).astype(
                jnp.bfloat16
            )
        sums_row = lax.dot_general(
            jnp.ones((8, 128), jnp.float32),
            squares,
            (((1,), (1,)), ((), ())),
            precision=highest,
        )
        ss_ref[2 * model : 2 * model + 1, :] = sums_row[0:1, :128]
        ss_ref[2 * model + 1 : 2 * model + 2, :] = sums_row[0:1, 128:]

    inside(0)
    join_pair(0)
    inside(1)
    join_pair(1)
    send_weights(0, (2,))
    g_copy.wait()
    for copy in decay_copies:
        copy.wait_recv()
    ss_ref[...] = jnp.zeros_like(ss_ref)

    token_in = {}
    token_own = []
    size = YS

    def send_tokens(model):
        at = token_at(model)
        mine = pl.ds(pl.multiple_of(c * rows, rows), rows)
        theirs = pl.ds(pl.multiple_of(other * rows, rows), rows)
        own = pltpu.make_async_copy(n_ref.at[model, mine], nf.at[model, c, at], local.at[3 + model])
        own.start()
        token_own.append(own)
        first = copies.take(8)
        to_sibling = start(
            copies.remote(n_ref.at[model, theirs], nf.at[model, c, at], first + 4, sibling)
        )
        sends = []
        for core in (0, 1):
            for n, step in ((0, 1), (1, -1)):
                piece = n_ref.at[model, pl.ds(core * rows, rows)]
                copy = pltpu.make_async_remote_copy(
                    src_ref=piece,
                    dst_ref=nf.at[model, c, at],
                    send_sem=send.at[first + 2 * core + n],
                    recv_sem=recv.at[first + 2 * c + n],
                    device_id=token_peer(model, step, core),
                    device_id_type=MESH,
                )
                sends.append(start(copy))
        token_in[model] = (first, to_sibling)

    def arrival(dst, slot):
        return copies.remote(dst, dst, slot, sibling)

    sibling_waits = []
    opposite = []

    def forward_weights(model, which):
        at = weight_at(model)
        for step, part_rows, n, copy in [w[1:] for w in weights_in if w[0] == model]:
            if n not in which:
                continue
            source = (at - step + size) % size
            copy.wait_recv()
            held = wf.at[model, source, c, part_rows]
            if n < 2:
                onward = start(
                    copies.remote(held, held, copies.take(), weight_peer(model, step))
                )
                opposite.append((model, step, part_rows, onward))
            sibling_waits.append(start(copies.remote(held, held, copies.take(), sibling)))

    def forward_opposite():
        for model, step, part_rows, onward in opposite:
            at = weight_at(model)
            source = (at - 2 * step + 2 * size) % size
            onward.wait_recv()
            held = wf.at[model, source, c, part_rows]
            sibling_waits.append(start(copies.remote(held, held, copies.take(), sibling)))

    token_forward = {}

    def forward_tokens(model):
        at = token_at(model)
        first, to_sibling = token_in[model]
        forwards = []
        for core, n, step in ((0, 0, 1), (1, 1, -1), (1, 0, 1), (0, 1, -1)):
            source = (at - step + size) % size
            arrival(nf.at[model, core, source], first + 2 * core + n).wait_recv()
            if core == n:
                forwards.append(
                    start(
                        copies.remote(
                            nf.at[model, core, source],
                            nf.at[model, core, source],
                            first + 5 + n,
                            token_peer(model, step, c),
                        )
                    )
                )
        token_forward[model] = (to_sibling, forwards)

    forward_weights(1, (0, 1))
    forward_weights(0, (1,))
    forward_weights(1, (2, 3))
    forward_weights(0, (3,))
    gate(0)
    send_tokens(0)
    gate(1)
    send_tokens(1)
    sums_first = copies.take(16)
    sums_local = pltpu.make_async_copy(ss_ref, sums.at[head], local.at[2])
    sums_sent = []
    for i in range(16):
        copy = pltpu.make_async_remote_copy(
            src_ref=ss_ref,
            dst_ref=sums.at[head],
            send_sem=send.at[sums_first + i],
            recv_sem=recv.at[sums_first + head],
            device_id={"seq": (seq + i) % 16, "head": seq},
            device_id_type=MESH,
        )
        sums_sent.append(copy)
        if i == 0:
            pl.when(head != seq)(copy.start)
            pl.when(head == seq)(sums_local.start)
        else:
            copy.start()

    forward_weights(0, (0,))
    forward_tokens(0)
    forward_weights(0, (2,))
    forward_tokens(1)
    forward_opposite()
    for own in own_local:
        own.wait()
    for copy in forward_later + sibling_waits:
        copy.wait_recv()

    def piece(model, z_to, e):
        if model == 0:
            return part.at[0, z_to // 2, 2 * (z_to % 2) + e]
        return part.at[1, 2 * (z_to % 2) + e, z_to // 2]

    ring_first = copies.take(28)
    sent_ring = {}

    def ring_step(model, k):
        for e, step in ((0, 1), (1, -1)):
            z_to = (z - step * (1 + k) + 2 * ZS) % ZS
            if k == 0:
                src = piece(model, z_to, e)
            else:
                sent_ring[model, e, k - 1].wait_recv()
                src = ring.at[model, e, k - 1]
                src[...] = (
                    src[...].astype(jnp.float32) + piece(model, z_to, e)[...].astype(jnp.float32)
                ).astype(src.dtype)
            copy = start(
                copies.remote(
                    src,
                    ring.at[model, e, k],
                    ring_first + 14 * model + 7 * e + k,
                    device(x, y, (z + step + ZS) % ZS, c),
                )
            )
            sent_ring[model, e, k] = copy

    def multiply(model, j):
        total = None
        for core in (0, 1):
            tokens = nf[model, core].reshape(4 * rows, nf.shape[4])
            term = jnp.dot(tokens, wf[model, j, core], preferred_element_type=jnp.float32)
            total = term if total is None else total + term
        part[model, :, j] = total.reshape(4, rows, total.shape[1]).astype(part.dtype)

    fin_first = copies.take(8)
    finals = []

    def finish(model):
        for e in (0, 1):
            sent_ring[model, e, 6].wait_recv()
            fin_src[model, e] = (
                ring[model, e, 6].astype(jnp.float32)
                + piece(model, z, e)[...].astype(jnp.float32)
            ).astype(fin_src.dtype)
            if model == 0:
                target = device(x, 2 * (z % 2) + e, 2 * (z // 2) + y // 2, y % 2)
                is_self = jnp.logical_and(
                    jnp.logical_and(z % 2 == y // 2, c == y % 2), y % 2 == e
                )
            else:
                target = device(z // 2, y, 2 * x + z % 2, e)
                is_self = jnp.logical_and(z // 2 == x, c == e)
            copy = pltpu.make_async_remote_copy(
                src_ref=fin_src.at[model, e],
                dst_ref=fin.at[model, c],
                send_sem=send.at[fin_first + 4 * model + e],
                recv_sem=recv.at[fin_first + 4 * model + c],
                device_id=target,
                device_id_type=MESH,
            )
            here = pltpu.make_async_copy(
                fin_src.at[model, e], fin.at[model, c], local.at[5 + 2 * model + e]
            )
            pl.when(jnp.logical_not(is_self))(copy.start)
            pl.when(is_self)(here.start)
            finals.append((is_self, copy, here))

    for model in (0, 1):
        first, to_sibling = token_in[model]
        to_sibling, forwards = token_forward[model]
        token_own[model].wait()
        to_sibling.wait_recv()
        for copy in forwards:
            copy.wait_recv()
        for j in range(4):
            multiply(model, j)
            if model == 1 and j % 2 == 1:
                ring_step(0, (j + 1) // 2)
        ring_step(model, 0)

    for k in range(3, 7):
        ring_step(0, k)
        ring_step(1, k - 2)
    finish(0)
    ring_step(1, 5)
    ring_step(1, 6)

    for i in range(16):
        here = jnp.logical_and(seq == head, head == i)
        arrived = pltpu.make_async_remote_copy(
            src_ref=ss_ref,
            dst_ref=sums.at[i],
            send_sem=send.at[sums_first + i],
            recv_sem=recv.at[sums_first + i],
            device_id=sibling,
            device_id_type=MESH,
        )
        pl.when(here)(sums_local.wait)
        pl.when(jnp.logical_not(here))(arrived.wait_recv)
    mean_square = jnp.sum(sums[...], axis=0) / 16384.0
    scale = lax.rsqrt(mean_square + 1e-05)
    columns = jnp.concatenate([scale] * 16, axis=0).T

    finish(1)
    for model in (0, 1):
        for core in (0, 1):
            if model == 0:
                from_self = jnp.logical_and(
                    jnp.logical_and(z % 2 == y // 2, c == y % 2), c == core
                )
                e = y % 2
            else:
                from_self = jnp.logical_and(z // 2 == x, c == core)
                e = c
            arrived = copies.remote(
                fin_src.at[model, 0], fin.at[model, core], fin_first + 4 * model + core, sibling
            )
            pl.when(jnp.logical_not(from_self))(arrived.wait_recv)

            @pl.when(from_self)
            def _():
                pltpu.make_async_copy(
                    fin_src.at[model, 0], fin.at[model, core], local.at[5 + 2 * model + e]
                ).wait()

            out_ref[model, core * rows : (core + 1) * rows] = (
                fin[model, core].astype(jnp.float32)
                * columns[:, 2 * model + core : 2 * model + core + 1]
            ).astype(out_ref.dtype)

    for copy in started:
        copy.wait_send()
    for i, copy in enumerate(sums_sent):
        if i == 0:
            pl.when(head != seq)(copy.wait_send)
        else:
            copy.wait_send()
    for is_self, copy, here in finals:
        pl.when(jnp.logical_not(is_self))(copy.wait_send)


def local(
    x_heads, gate_z, b_proj, c_proj, dt_raw, dt_bias, decay_rate, skip_d, norm_gain, w_out, seg_ids
):
    tokens, lanes = x_heads.shape[1], x_heads.shape[2]
    depth, width = w_out.shape[1], w_out.shape[2]
    state, rows = b_proj.shape[2], tokens // 2
    bf16, f32 = jnp.bfloat16, jnp.float32
    vmem = pl.BlockSpec(memory_space=pltpu.VMEM)
    hbm = pl.BlockSpec(memory_space=pl.ANY)
    count = 128
    return pl.pallas_call(
        layer_kernel,
        out_shape=jax.ShapeDtypeStruct((2, tokens, width), bf16),
        in_specs=[hbm, hbm] + [vmem] * 8 + [hbm],
        out_specs=vmem,
        scratch_shapes=[
            pltpu.VMEM((2, tokens, lanes), bf16),
            pltpu.VMEM((2, tokens, lanes), bf16),
            pltpu.VMEM((2, tokens, lanes), bf16),
            pltpu.VMEM((8, 128), f32),
            pltpu.VMEM((2, tokens, lanes), f32),
            pltpu.VMEM((tokens, tokens), f32),
            pltpu.VMEM((tokens, tokens), f32),
            pltpu.VMEM((dt_raw.shape[2], lanes), bf16),
            pltpu.VMEM((8, tokens), f32),
            pltpu.VMEM((8, tokens), f32),
            pltpu.VMEM((2, state, lanes), f32),
            pltpu.VMEM((2, state, lanes), bf16),
            pltpu.VMEM((2, state, lanes), bf16),
            pltpu.VMEM((2, state, lanes), bf16),
            pltpu.VMEM((2, 2, state, lanes), bf16),
            pltpu.VMEM((2, 8, lanes), f32),
            pltpu.VMEM((2, 2, 8, lanes), f32),
            pltpu.VMEM((2, 4, 2, depth, width), bf16),
            pltpu.VMEM((2, 2, 4, rows, depth), bf16),
            pltpu.VMEM((2, 4, 4, rows, width), bf16),
            pltpu.VMEM((2, 2, 7, rows, width), bf16),
            pltpu.VMEM((2, 2, rows, width), bf16),
            pltpu.VMEM((2, 2, rows, width), bf16),
            pltpu.VMEM((16, 8, 128), f32),
            pltpu.SemaphoreType.DMA((count,)),
            pltpu.SemaphoreType.DMA((count,)),
            pltpu.SemaphoreType.DMA((11,)),
        ],
        compiler_params=pltpu.CompilerParams(
            has_side_effects=True, vmem_limit_bytes=62 * 1024 * 1024
        ),
    )(
        x_heads,
        gate_z,
        b_proj,
        c_proj,
        dt_raw,
        dt_bias,
        decay_rate,
        skip_d,
        norm_gain,
        seg_ids.reshape(1, tokens),
        w_out,
    )


def solution(mesh):
    placed = (
        P(None, "seq", "head"),
        P(None, "seq", "head"),
        P(None, "seq", None),
        P(None, "seq", None),
        P(None, "seq", "head"),
        P(None, "head"),
        P(None, "head"),
        P(None, "head"),
        P(None, "head"),
        P(None, "head", "seq"),
        P("seq"),
    )
    return jax.shard_map(
        local, mesh=mesh, in_specs=placed, out_specs=P(None, "head", "seq"), check_vma=False
    )
```

```python
import functools

import jax
import jax.numpy as jnp
from jax import lax
from jax.experimental import pallas as pl
from jax.experimental.pallas import tpu as pltpu
from jax.sharding import PartitionSpec as P

highest = lax.Precision.HIGHEST
FAR = -1e30

MESH = pl.DeviceIdType.MESH
XS, YS, ZS = 4, 4, 8


class Copies:
    def __init__(self, send, recv):
        self.send, self.recv, self.used = send, recv, 0

    def take(self, count=1):
        first = self.used
        self.used += count
        return first

    def remote(self, src, dst, slot, device):
        return pltpu.make_async_remote_copy(
            src_ref=src,
            dst_ref=dst,
            send_sem=self.send.at[slot],
            recv_sem=self.recv.at[slot],
            device_id=device,
            device_id_type=MESH,
        )


def layer_kernel(
    x_hbm, g_hbm, b_ref, c_ref, dt_ref, bias_ref, rate_ref, skip_ref, gain_ref, seg_ref, w_ref,
    out_ref,
    xv, gv, n_ref, ss_ref, inner, mask, products, spread, seg_own, seg_before,
    local_state, state_out, state_in, pair_out, pair_in, decay_own, decay_two,
    wf, nf, part, ring, fin_src, fin, sums, send, recv, local,
):
    seq, head = lax.axis_index("seq"), lax.axis_index("head")
    x, y = seq // YS, seq % YS
    z, c = head // 2, head % 2
    other = 1 - c

    def device(x_at, y_at, z_at, c_at):
        return {"seq": x_at * YS + y_at, "head": z_at * 2 + c_at}

    copies = Copies(send, recv)
    started = []

    def start(copy):
        copy.start()
        started.append(copy)
        return copy

    sibling = device(x, y, z, other)

    def weight_peer(step):
        return device(x, (y + step) % YS, z, c)

    def token_peer(step, core):
        return device((x + step) % XS, y, z, core)

    half = wf.shape[3] // 2
    rows = nf.shape[3]
    tokens, lanes = xv.shape[1], xv.shape[2]
    heads = dt_ref.shape[1]
    upper, lower = pl.ds(0, half), pl.ds(half, half)

    x_copy = pltpu.make_async_copy(x_hbm, xv, local.at[9])
    g_copy = pltpu.make_async_copy(g_hbm, gv, local.at[10])
    x_copy.start()

    def follower(distance):
        return {"seq": (seq + distance) % 16, "head": head}

    barrier = pltpu.get_barrier_semaphore()

    def greet(target):
        pl.semaphore_signal(barrier, inc=1, device_id=target, device_id_type=MESH)

    greet(sibling)
    for step in (1, -1):
        for core in (0, 1):
            greet(device((x + step + XS) % XS, y, z, core))
            greet(device(x, (y + step + YS) % YS, z, core))
        greet(device(x, y, (z + step + ZS) % ZS, c))
    for distance in (1, 2, 3):
        greet(follower(16 - distance))
    stays = jnp.logical_and(z % 2 == y // 2, c == y % 2)
    for core in (0, 1):
        pl.when(jnp.logical_not(jnp.logical_and(stays, c == core)))(
            functools.partial(
                greet, device(x, 2 * (z % 2) + c, 2 * (z // 2) + y // 2, core)
            )
        )
    for i in range(16):
        pl.when(jnp.logical_not(jnp.logical_and(seq == head, head == i)))(
            functools.partial(greet, {"seq": head, "head": i})
        )
    greeted = 32 - stays.astype(jnp.int32) - (seq == head).astype(jnp.int32)

    seg_row = seg_ref[...].astype(jnp.float32)
    seg_own[...] = jnp.broadcast_to(seg_row, seg_own.shape)

    arrived = {}
    size = YS
    own_local = []
    weight_slot = [copies.take(5) for model in (0, 1)]
    order = ((1, upper, 0), (-1, lower, 1), (1, lower, 2), (-1, upper, 3))

    def send_weights(model, which):
        at = y
        for step, part_rows, n in order:
            if n in which:
                copy = start(
                    copies.remote(
                        w_ref.at[model, part_rows],
                        wf.at[model, at, c, part_rows],
                        weight_slot[model] + n,
                        weight_peer(step),
                    )
                )
                arrived[model, n] = copy

    g_copy.start()
    forward_later = {}
    for model in (0, 1):
        at = y
        own = pltpu.make_async_copy(w_ref.at[model], wf.at[model, at, c], local.at[model])
        own.start()
        own_local.append(own)

    def share_own(model):
        forward_later[model] = start(
            copies.remote(
                w_ref.at[model],
                wf.at[model, y, c],
                weight_slot[model] + 4,
                sibling,
            )
        )

    row_at = lax.broadcasted_iota(jnp.int32, (tokens, tokens), 0)
    col_at = lax.broadcasted_iota(jnp.int32, (tokens, tokens), 1)
    eye = (row_at == col_at).astype(jnp.float32)
    lower_ones = (row_at >= col_at).astype(jnp.float32)
    seg_col = lax.dot_general(
        eye, seg_own[...], (((1,), (1,)), ((), ())), precision=highest
    )[:, 0:1]
    mask[...] = jnp.where(
        jnp.logical_and(row_at >= col_at, jnp.abs(seg_col - seg_row) < 0.5), 0.0, FAR
    )
    spread[...] = (
        lax.broadcasted_iota(jnp.int32, spread.shape, 0)
        == lax.broadcasted_iota(jnp.int32, spread.shape, 1) // (lanes // heads)
    ).astype(spread.dtype)
    same_last = (jnp.abs(seg_col - seg_row[:, tokens - 1 : tokens]) < 0.5).astype(jnp.float32)

    def widen(values, columns):
        coarse = values.astype(jnp.bfloat16)
        fine = (values - coarse.astype(jnp.float32)).astype(jnp.bfloat16)
        table = spread[:, columns]
        return jnp.dot(coarse, table, preferred_element_type=jnp.float32) + jnp.dot(
            fine, table, preferred_element_type=jnp.float32
        )

    blocks = [pl.ds(start_at, 256) for start_at in range(0, lanes, 256)]
    state_first = copies.take(2)
    state_copies, running, shifted, totals, tails = {}, {}, {}, {}, {}
    for model in (1, 0):
        raw = (
            lax.dot_general(eye, dt_ref[model], (((1,), (1,)), ((), ())), precision=highest)
            + bias_ref[model : model + 1, :]
        )
        step_size = jnp.maximum(raw, 0.0) + jnp.log1p(jnp.exp(-jnp.abs(raw)))
        log_decay = -(rate_ref[model : model + 1, :] * step_size)
        run = jnp.dot(lower_ones, log_decay, precision=highest)
        total = run[tokens - 1 : tokens, :]
        tails[model] = jnp.exp(total - run) * same_last * step_size
        running[model] = run
        totals[model] = total
        shifted[model] = run - jnp.log(step_size)
        seg_own[1 + model : 2 + model, 0:heads] = total

    def own_state(model):
        for block in blocks:
            weighted = (
                xv[model, :, block].astype(jnp.float32) * widen(tails[model], block)
            ).astype(jnp.bfloat16)
            fresh = lax.dot_general(
                b_ref[model],
                weighted,
                (((0,), (0,)), ((), ())),
                preferred_element_type=jnp.float32,
            )
            local_state[model, :, block] = fresh
            state_out[model, :, block] = fresh.astype(jnp.bfloat16)

    def send_state(model):
        state_copies[model] = start(
            copies.remote(
                state_out.at[model], state_in.at[model], state_first + model, follower(1)
            )
        )

    x_copy.wait()
    own_state(1)
    pl.semaphore_wait(barrier, greeted)
    info_first = copies.take(3)
    info_copies = [
        start(copies.remote(seg_own, seg_before.at[i], info_first + i, follower(i + 1)))
        for i in range(3)
    ]
    send_state(1)
    send_weights(1, (1,))
    own_state(0)
    send_state(0)
    share_own(1)
    share_own(0)

    for copy in info_copies:
        copy.wait_recv()

    def last_of(block_at):
        if block_at == 0:
            return seg_row[:, tokens - 1 : tokens]
        return seg_before[block_at - 1, 0:1, tokens - 1 : tokens]

    def decay_over(block_at, model, total):
        present = jnp.where(seq > block_at, 1.0, 0.0)
        same = (jnp.abs(last_of(block_at) - last_of(block_at + 1)) < 0.5).astype(jnp.float32)
        return jnp.exp(total) * same * present

    entered = (jnp.abs(seg_col - last_of(1)) < 0.5).astype(jnp.float32) * jnp.where(
        seq > 0, 1.0, 0.0
    )
    for model in (1, 0):
        near_decay = decay_over(0, model, totals[model])
        two = decay_over(1, model, seg_before[0, 1 + model : 2 + model, 0:heads]) * decay_over(
            2, model, seg_before[1, 1 + model : 2 + model, 0:heads]
        )
        for block in blocks:
            decay_own[model : model + 1, block] = widen(
                jnp.broadcast_to(near_decay, (8, heads)), block
            )[0:1, :]
            decay_two[model : model + 1, block] = widen(
                jnp.broadcast_to(two, (8, heads)), block
            )[0:1, :]

    def inside(model):
        run = running[model]
        shifted_t = lax.dot_general(
            shifted[model], eye, (((0,), (0,)), ((), ())), precision=highest
        )
        products[...] = lax.dot_general(
            c_ref[model],
            b_ref[model],
            (((1,), (1,)), ((), ())),
            preferred_element_type=jnp.float32,
        )
        lane = lax.broadcasted_iota(jnp.int32, (1, 128), 1)
        skip = jnp.broadcast_to(skip_ref[model : model + 1, :], (8, heads))
        mid = tokens // 2
        for pair in range(heads // 2):
            columns = pl.ds(128 * pair, 128)
            x_pair = xv[model, :, columns]
            early = late = None
            for q in (0, 1):
                h = 2 * pair + q
                x_one = x_pair * (lane // 64 == q).astype(jnp.bfloat16)
                gap = run[:mid, h : h + 1] - shifted_t[h : h + 1, :mid] + mask[:mid, :mid]
                weights = (jnp.exp(gap) * products[:mid, :mid]).astype(jnp.bfloat16)
                term = jnp.dot(weights, x_one[:mid], preferred_element_type=jnp.float32)
                early = term if early is None else early + term
                gap = run[mid:, h : h + 1] - shifted_t[h : h + 1, :] + mask[mid:, :]
                weights = (jnp.exp(gap) * products[mid:, :]).astype(jnp.bfloat16)
                term = jnp.dot(weights, x_one, preferred_element_type=jnp.float32)
                late = term if late is None else late + term
            passed = x_pair.astype(jnp.float32) * widen(skip, columns)[0:1, :]
            inner[model, :mid, columns] = early + passed[:mid]
            inner[model, mid:, columns] = late + passed[mid:]

    pair_first = copies.take(4)
    pair_copies = {}

    def join_pair(model):
        state_copies[model].wait_recv()
        for block in blocks:
            pair_out[model, :, block] = (
                local_state[model, :, block]
                + decay_own[model : model + 1, block] * state_in[model, :, block].astype(jnp.float32)
            ).astype(jnp.bfloat16)
        pair_copies[model] = [
            start(
                copies.remote(
                    pair_out.at[model],
                    pair_in.at[model, i],
                    pair_first + 2 * model + i,
                    follower(1 + 2 * i),
                )
            )
            for i in (1, 0)
        ]

    def gate(model):
        entry_w = jnp.exp(running[model]) * entered
        squares = jnp.zeros((tokens, 128), jnp.float32)
        for copy in pair_copies[model]:
            copy.wait_recv()
        for block in blocks:
            earlier = pair_in[model, 0, :, block].astype(jnp.float32) + decay_two[
                model : model + 1, block
            ] * pair_in[model, 1, :, block].astype(jnp.float32)
            entering = jnp.dot(
                c_ref[model], earlier.astype(jnp.bfloat16), preferred_element_type=jnp.float32
            )
            ssd_out = inner[model, :, block] + widen(entry_w, block) * entering
            opened = gv[model, :, block].astype(jnp.float32)
            gated = ssd_out * (opened / (1.0 + jnp.exp(-opened)))
            squares = squares + (
                gated[:, :128] * gated[:, :128] + gated[:, 128:] * gated[:, 128:]
            )
            n_ref[model, :, block] = (gated * gain_ref[model : model + 1, block]).astype(
                jnp.bfloat16
            )
        sums_row = lax.dot_general(
            jnp.ones((8, 128), jnp.float32),
            squares,
            (((1,), (1,)), ((), ())),
            precision=highest,
        )
        ss_ref[2 * model : 2 * model + 1, :] = sums_row[0:1, :128]
        ss_ref[2 * model + 1 : 2 * model + 2, :] = sums_row[0:1, 128:]

    inside(1)
    join_pair(1)
    inside(0)
    join_pair(0)
    send_weights(1, (3, 0, 2))
    send_weights(0, (0, 2))
    g_copy.wait()
    ss_ref[...] = jnp.zeros_like(ss_ref)

    token_in = {}
    token_own = {}

    def send_tokens(model):
        at = x
        mine = pl.ds(pl.multiple_of(c * rows, rows), rows)
        theirs = pl.ds(pl.multiple_of(other * rows, rows), rows)
        own = pltpu.make_async_copy(n_ref.at[model, mine], nf.at[model, c, at], local.at[3 + model])
        own.start()
        token_own[model] = own
        first = copies.take(8)
        to_sibling = start(
            copies.remote(n_ref.at[model, theirs], nf.at[model, c, at], first + 4, sibling)
        )
        sends = []
        for core in (0, 1):
            for n, step in ((0, 1), (1, -1)):
                piece = n_ref.at[model, pl.ds(core * rows, rows)]
                copy = pltpu.make_async_remote_copy(
                    src_ref=piece,
                    dst_ref=nf.at[model, c, at],
                    send_sem=send.at[first + 2 * core + n],
                    recv_sem=recv.at[first + 2 * c + n],
                    device_id=token_peer(step, core),
                    device_id_type=MESH,
                )
                sends.append(start(copy))
        token_in[model] = (first, to_sibling)

    def arrival(dst, slot):
        return copies.remote(dst, dst, slot, sibling)

    shared = {}
    onward = {1: (1, 3), 0: (0, 1)}

    def forward_weights(model, n):
        at = y
        step, part_rows = order[n][0], order[n][1]
        source = (at - step + size) % size
        arrived[model, n].wait_recv()
        held = wf.at[model, source, c, part_rows]
        if n in onward[model]:
            shared[model, n, "on"] = start(
                copies.remote(held, held, copies.take(), weight_peer(step))
            )
        shared[model, n, "near"] = start(copies.remote(held, held, copies.take(), sibling))

    def forward_opposite(model, n):
        part_rows = order[n][1]
        source = (y + 2) % size
        shared[model, n, "on"].wait_recv()
        held = wf.at[model, source, c, part_rows]
        shared[model, n, "far"] = start(copies.remote(held, held, copies.take(), sibling))

    token_forward = {}

    def forward_tokens(model):
        at = x
        first, to_sibling = token_in[model]
        forwards = []
        for core, n, step in ((0, 0, 1), (1, 1, -1), (1, 0, 1), (0, 1, -1)):
            source = (at - step + size) % size
            arrival(nf.at[model, core, source], first + 2 * core + n).wait_recv()
            if core == n:
                forwards.append(
                    start(
                        copies.remote(
                            nf.at[model, core, source],
                            nf.at[model, core, source],
                            first + 5 + n,
                            token_peer(step, c),
                        )
                    )
                )
        token_forward[model] = (to_sibling, forwards)

    forward_weights(1, 1)
    gate(1)
    send_tokens(1)
    gate(0)
    forward_weights(1, 3)
    send_weights(0, (1, 3))
    forward_tokens(1)
    send_tokens(0)
    sums_first = copies.take(16)
    sums_local = pltpu.make_async_copy(ss_ref, sums.at[head], local.at[2])
    sums_sent = []
    for i in range(16):
        copy = pltpu.make_async_remote_copy(
            src_ref=ss_ref,
            dst_ref=sums.at[head],
            send_sem=send.at[sums_first + i],
            recv_sem=recv.at[sums_first + head],
            device_id={"seq": (seq + i) % 16, "head": seq},
            device_id_type=MESH,
        )
        sums_sent.append(copy)
        if i == 0:
            pl.when(head != seq)(copy.start)
            pl.when(head == seq)(sums_local.start)
        else:
            copy.start()

    forward_weights(1, 0)
    forward_weights(1, 2)
    forward_opposite(1, 1)

    def piece(model, z_to, e):
        return part.at[model, (2 * (z_to % 2) + e - y + 4) % 4, z_to // 2]

    ring_first = copies.take(112)
    sent_ring = {}
    thin = rows // 4

    def ring_step(model, k, late):
        e = y % 2 if late else 1 - y % 2
        for v in (0, 1):
            for u, step in ((0, 1), (1, -1)):
                strip = pl.ds((2 * u + v) * thin, thin)
                z_to = (z - step * (1 + k) + 2 * ZS) % ZS
                if k == 0:
                    src = piece(model, z_to, e).at[strip]
                else:
                    sent_ring[model, late, u, v, k - 1].wait_recv()
                    src = ring.at[model, late, k - 1, strip]
                    src[...] = (
                        src[...].astype(jnp.float32)
                        + piece(model, z_to, e)[strip].astype(jnp.float32)
                    ).astype(src.dtype)
                sent_ring[model, late, u, v, k] = start(
                    copies.remote(
                        src,
                        ring.at[model, late, k, strip],
                        ring_first + 56 * model + 28 * late + 14 * u + 7 * v + k,
                        device(x, y, (z + step + ZS) % ZS, c),
                    )
                )

    def multiply(model, j, t):
        total = None
        for core in (0, 1):
            tokens = nf[model, core].reshape(4 * rows, nf.shape[4])
            term = jnp.dot(tokens, wf[model, j, core], preferred_element_type=jnp.float32)
            total = term if total is None else total + term
        part[model, t] = total.reshape(4, rows, total.shape[1]).astype(part.dtype)

    fin_first = copies.take(8)
    finals = []

    def finish(model):
        for late in (0, 1):
            e = y % 2 if late else 1 - y % 2
            for u in (0, 1):
                for v in (0, 1):
                    sent_ring[model, late, u, v, 6].wait_recv()
            fin_src[model, late] = (
                ring[model, late, 6].astype(jnp.float32)
                + piece(model, z, e)[...].astype(jnp.float32)
            ).astype(fin_src.dtype)
            target = device(x, 2 * (z % 2) + e, 2 * (z // 2) + y // 2, y % 2)
            copy = pltpu.make_async_remote_copy(
                src_ref=fin_src.at[model, late],
                dst_ref=fin.at[model, c],
                send_sem=send.at[fin_first + 4 * model + late],
                recv_sem=recv.at[fin_first + 4 * model + c],
                device_id=target,
                device_id_type=MESH,
            )
            if late:
                here = pltpu.make_async_copy(
                    fin_src.at[model, late], fin.at[model, c], local.at[5 + model]
                )
                pl.when(jnp.logical_not(stays))(copy.start)
                pl.when(stays)(here.start)
                finals.append(copy)
            else:
                start(copy)

    def tokens_ready(model):
        to_sibling, forwards = token_forward[model]
        token_own[model].wait()
        to_sibling.wait_recv()
        for copy in forwards:
            copy.wait_recv()

    def product(model, t):
        at = y
        if t == 0:
            own_local[model].wait()
            forward_later[model].wait_recv()
        elif t == 1:
            shared[model, 1, "near"].wait_recv()
            shared[model, 3, "near"].wait_recv()
        elif t == 3:
            shared[model, 0, "near"].wait_recv()
            shared[model, 2, "near"].wait_recv()
        else:
            for n in onward[model]:
                shared[model, n, "far"].wait_recv()
        multiply(model, (at + t) % 4, t)

    tokens_ready(1)
    product(1, 0)
    product(1, 1)
    product(1, 3)
    ring_step(1, 0, 0)
    forward_opposite(1, 3)
    ring_step(1, 1, 0)
    product(1, 2)
    ring_step(1, 0, 1)
    forward_weights(0, 0)
    ring_step(1, 2, 0)
    ring_step(1, 1, 1)
    forward_tokens(0)
    ring_step(1, 3, 0)
    ring_step(1, 2, 1)
    forward_weights(0, 1)
    ring_step(1, 4, 0)
    ring_step(1, 3, 1)
    forward_weights(0, 2)
    tokens_ready(0)
    product(0, 0)
    ring_step(1, 5, 0)
    ring_step(1, 4, 1)
    ring_step(1, 6, 0)
    ring_step(1, 5, 1)
    forward_weights(0, 3)
    product(0, 3)
    ring_step(1, 6, 1)
    product(0, 1)
    ring_step(0, 0, 0)
    finish(1)
    forward_opposite(0, 0)
    ring_step(0, 1, 0)
    ring_step(0, 2, 0)
    forward_opposite(0, 1)
    product(0, 2)
    ring_step(0, 0, 1)
    for k in range(3, 7):
        ring_step(0, k, 0)
        ring_step(0, k - 2, 1)
    ring_step(0, 5, 1)
    ring_step(0, 6, 1)

    for i in range(16):
        here = jnp.logical_and(seq == head, head == i)
        arrived = pltpu.make_async_remote_copy(
            src_ref=ss_ref,
            dst_ref=sums.at[i],
            send_sem=send.at[sums_first + i],
            recv_sem=recv.at[sums_first + i],
            device_id=sibling,
            device_id_type=MESH,
        )
        pl.when(here)(sums_local.wait)
        pl.when(jnp.logical_not(here))(arrived.wait_recv)
    mean_square = jnp.sum(sums[...], axis=0) / 16384.0
    scale = lax.rsqrt(mean_square + 1e-05)
    columns = jnp.concatenate([scale] * 16, axis=0).T

    finish(0)
    for model in (1, 0):
        for core in (0, 1):
            from_self = jnp.logical_and(stays, c == core)
            landed = copies.remote(
                fin_src.at[model, 0], fin.at[model, core], fin_first + 4 * model + core, sibling
            )
            pl.when(jnp.logical_not(from_self))(landed.wait_recv)

            @pl.when(from_self)
            def _():
                pltpu.make_async_copy(
                    fin_src.at[model, 0], fin.at[model, core], local.at[5 + model]
                ).wait()

            out_ref[model, core * rows : (core + 1) * rows] = (
                fin[model, core].astype(jnp.float32)
                * columns[:, 2 * model + core : 2 * model + core + 1]
            ).astype(out_ref.dtype)

    for copy in started:
        copy.wait_send()
    for i, copy in enumerate(sums_sent):
        if i == 0:
            pl.when(head != seq)(copy.wait_send)
        else:
            copy.wait_send()
    for copy in finals:
        pl.when(jnp.logical_not(stays))(copy.wait_send)


def local(
    x_heads, gate_z, b_proj, c_proj, dt_raw, dt_bias, decay_rate, skip_d, norm_gain, w_out, seg_ids
):
    tokens, lanes = x_heads.shape[1], x_heads.shape[2]
    depth, width = w_out.shape[1], w_out.shape[2]
    state, rows = b_proj.shape[2], tokens // 2
    bf16, f32 = jnp.bfloat16, jnp.float32
    vmem = pl.BlockSpec(memory_space=pltpu.VMEM)
    hbm = pl.BlockSpec(memory_space=pl.ANY)
    count = 232
    return pl.pallas_call(
        layer_kernel,
        out_shape=jax.ShapeDtypeStruct((2, tokens, width), bf16),
        in_specs=[hbm, hbm] + [vmem] * 8 + [hbm],
        out_specs=vmem,
        scratch_shapes=[
            pltpu.VMEM((2, tokens, lanes), bf16),
            pltpu.VMEM((2, tokens, lanes), bf16),
            pltpu.VMEM((2, tokens, lanes), bf16),
            pltpu.VMEM((8, 128), f32),
            pltpu.VMEM((2, tokens, lanes), f32),
            pltpu.VMEM((tokens, tokens), f32),
            pltpu.VMEM((tokens, tokens), f32),
            pltpu.VMEM((dt_raw.shape[2], lanes), bf16),
            pltpu.VMEM((8, tokens), f32),
            pltpu.VMEM((3, 8, tokens), f32),
            pltpu.VMEM((2, state, lanes), f32),
            pltpu.VMEM((2, state, lanes), bf16),
            pltpu.VMEM((2, state, lanes), bf16),
            pltpu.VMEM((2, state, lanes), bf16),
            pltpu.VMEM((2, 2, state, lanes), bf16),
            pltpu.VMEM((8, lanes), f32),
            pltpu.VMEM((8, lanes), f32),
            pltpu.VMEM((2, 4, 2, depth, width), bf16),
            pltpu.VMEM((2, 2, 4, rows, depth), bf16),
            pltpu.VMEM((2, 4, 4, rows, width), bf16),
            pltpu.VMEM((2, 2, 7, rows, width), bf16),
            pltpu.VMEM((2, 2, rows, width), bf16),
            pltpu.VMEM((2, 2, rows, width), bf16),
            pltpu.VMEM((16, 8, 128), f32),
            pltpu.SemaphoreType.DMA((count,)),
            pltpu.SemaphoreType.DMA((count,)),
            pltpu.SemaphoreType.DMA((11,)),
        ],
        compiler_params=pltpu.CompilerParams(
            collective_id=0, has_side_effects=True, vmem_limit_bytes=62 * 1024 * 1024
        ),
    )(
        x_heads,
        gate_z,
        b_proj,
        c_proj,
        jnp.transpose(dt_raw, (0, 2, 1)),
        dt_bias,
        decay_rate,
        skip_d,
        norm_gain,
        seg_ids.reshape(1, tokens),
        w_out,
    )


def solution(mesh):
    placed = (
        P(None, "seq", "head"),
        P(None, "seq", "head"),
        P(None, "seq", None),
        P(None, "seq", None),
        P(None, "seq", "head"),
        P(None, "head"),
        P(None, "head"),
        P(None, "head"),
        P(None, "head"),
        P(None, "head", "seq"),
        P("seq"),
    )
    return jax.shard_map(
        local, mesh=mesh, in_specs=placed, out_specs=P(None, "head", "seq"), check_vma=False
    )
```

```python
import functools

import jax
import jax.numpy as jnp
from jax import lax
from jax.experimental import pallas as pl
from jax.experimental.pallas import tpu as pltpu
from jax.sharding import PartitionSpec as P

highest = lax.Precision.HIGHEST
FAR = -1e30

MESH = pl.DeviceIdType.MESH
XS, YS, ZS = 4, 4, 8


class Copies:
    def __init__(self, send, recv):
        self.send, self.recv, self.used = send, recv, 0

    def take(self, count=1):
        first = self.used
        self.used += count
        return first

    def remote(self, src, dst, slot, device):
        return pltpu.make_async_remote_copy(
            src_ref=src,
            dst_ref=dst,
            send_sem=self.send.at[slot],
            recv_sem=self.recv.at[slot],
            device_id=device,
            device_id_type=MESH,
        )


def layer_kernel(
    x_hbm, g_hbm, b_ref, c_ref, dt_ref, bias_ref, rate_ref, skip_ref, gain_ref, seg_ref, w_ref,
    out_ref,
    xv, gv, n_ref, ss_ref, inner, mask, products, spread, seg_own, seg_before,
    local_state, state_out, state_in, pair_out, pair_in, decay_own, decay_two,
    wf, nf, part, ring, fin_src, fin, sums, send, recv, local,
):
    seq, head = lax.axis_index("seq"), lax.axis_index("head")
    x, y = seq // YS, seq % YS
    z, c = head // 2, head % 2
    other = 1 - c

    def device(x_at, y_at, z_at, c_at):
        return {"seq": x_at * YS + y_at, "head": z_at * 2 + c_at}

    copies = Copies(send, recv)
    started = []

    def start(copy):
        copy.start()
        started.append(copy)
        return copy

    sibling = device(x, y, z, other)

    def weight_peer(step):
        return device(x, (y + step) % YS, z, c)

    def token_peer(step, core):
        return device((x + step) % XS, y, z, core)

    half = wf.shape[3] // 2
    rows = nf.shape[3]
    tokens, lanes = xv.shape[1], xv.shape[2]
    heads = dt_ref.shape[1]
    upper, lower = pl.ds(0, half), pl.ds(half, half)

    x_copy = pltpu.make_async_copy(x_hbm, xv, local.at[9])
    g_copy = pltpu.make_async_copy(g_hbm, gv, local.at[10])
    x_copy.start()

    def follower(distance):
        return {"seq": (seq + distance) % 16, "head": head}

    barrier = pltpu.get_barrier_semaphore()

    def greet(target):
        pl.semaphore_signal(barrier, inc=1, device_id=target, device_id_type=MESH)

    greet(sibling)
    for step in (1, -1):
        for core in (0, 1):
            greet(device((x + step + XS) % XS, y, z, core))
            greet(device(x, (y + step + YS) % YS, z, core))
        greet(device(x, y, (z + step + ZS) % ZS, c))
    for distance in (1, 2, 3):
        greet(follower(16 - distance))
    stays = jnp.logical_and(z % 2 == y // 2, c == y % 2)
    for core in (0, 1):
        pl.when(jnp.logical_not(jnp.logical_and(stays, c == core)))(
            functools.partial(
                greet, device(x, 2 * (z % 2) + c, 2 * (z // 2) + y // 2, core)
            )
        )
    for i in range(16):
        pl.when(jnp.logical_not(jnp.logical_and(seq == head, head == i)))(
            functools.partial(greet, {"seq": head, "head": i})
        )
    greeted = 32 - stays.astype(jnp.int32) - (seq == head).astype(jnp.int32)

    seg_row = seg_ref[...].astype(jnp.float32)
    seg_own[...] = jnp.broadcast_to(seg_row, seg_own.shape)

    arrived = {}
    size = YS
    own_local = []
    weight_slot = [copies.take(5) for model in (0, 1)]
    order = ((1, upper, 0), (-1, lower, 1), (1, lower, 2), (-1, upper, 3))

    def send_weights(model, which):
        at = y
        for step, part_rows, n in order:
            if n in which:
                copy = start(
                    copies.remote(
                        w_ref.at[model, part_rows],
                        wf.at[model, at, c, part_rows],
                        weight_slot[model] + n,
                        weight_peer(step),
                    )
                )
                arrived[model, n] = copy

    g_copy.start()
    forward_later = {}
    for model in (0, 1):
        at = y
        own = pltpu.make_async_copy(w_ref.at[model], wf.at[model, at, c], local.at[model])
        own.start()
        own_local.append(own)

    def share_own(model):
        forward_later[model] = start(
            copies.remote(
                w_ref.at[model],
                wf.at[model, y, c],
                weight_slot[model] + 4,
                sibling,
            )
        )

    row_at = lax.broadcasted_iota(jnp.int32, (tokens, tokens), 0)
    col_at = lax.broadcasted_iota(jnp.int32, (tokens, tokens), 1)
    eye = (row_at == col_at).astype(jnp.float32)
    lower_ones = (row_at >= col_at).astype(jnp.float32)
    seg_col = lax.dot_general(
        eye, seg_own[...], (((1,), (1,)), ((), ())), precision=highest
    )[:, 0:1]
    mask[...] = jnp.where(
        jnp.logical_and(row_at >= col_at, jnp.abs(seg_col - seg_row) < 0.5), 0.0, FAR
    )
    spread[...] = (
        lax.broadcasted_iota(jnp.int32, spread.shape, 0)
        == lax.broadcasted_iota(jnp.int32, spread.shape, 1) // (lanes // heads)
    ).astype(spread.dtype)
    same_last = (jnp.abs(seg_col - seg_row[:, tokens - 1 : tokens]) < 0.5).astype(jnp.float32)

    def widen(values, columns):
        coarse = values.astype(jnp.bfloat16)
        fine = (values - coarse.astype(jnp.float32)).astype(jnp.bfloat16)
        table = spread[:, columns]
        return jnp.dot(coarse, table, preferred_element_type=jnp.float32) + jnp.dot(
            fine, table, preferred_element_type=jnp.float32
        )

    blocks = [pl.ds(start_at, 256) for start_at in range(0, lanes, 256)]
    state_first = copies.take(2)
    state_copies, running, shifted, totals, tails = {}, {}, {}, {}, {}
    for model in (1, 0):
        raw = (
            lax.dot_general(eye, dt_ref[model], (((1,), (1,)), ((), ())), precision=highest)
            + bias_ref[model : model + 1, :]
        )
        step_size = jnp.maximum(raw, 0.0) + jnp.log1p(jnp.exp(-jnp.abs(raw)))
        log_decay = -(rate_ref[model : model + 1, :] * step_size)
        run = jnp.dot(lower_ones, log_decay, precision=highest)
        total = run[tokens - 1 : tokens, :]
        tails[model] = jnp.exp(total - run) * same_last * step_size
        running[model] = run
        totals[model] = total
        shifted[model] = run - jnp.log(step_size)
        seg_own[1 + model : 2 + model, 0:heads] = total

    def own_state(model):
        for block in blocks:
            weighted = (
                xv[model, :, block].astype(jnp.float32) * widen(tails[model], block)
            ).astype(jnp.bfloat16)
            fresh = lax.dot_general(
                b_ref[model],
                weighted,
                (((0,), (0,)), ((), ())),
                preferred_element_type=jnp.float32,
            )
            local_state[model, :, block] = fresh
            state_out[model, :, block] = fresh.astype(jnp.bfloat16)

    def send_state(model):
        state_copies[model] = start(
            copies.remote(
                state_out.at[model], state_in.at[model], state_first + model, follower(1)
            )
        )

    x_copy.wait()
    own_state(1)
    pl.semaphore_wait(barrier, greeted)
    info_first = copies.take(3)
    info_copies = [
        start(copies.remote(seg_own, seg_before.at[i], info_first + i, follower(i + 1)))
        for i in range(3)
    ]
    send_state(1)
    send_weights(1, (1,))
    own_state(0)
    send_state(0)
    share_own(1)
    share_own(0)

    for copy in info_copies:
        copy.wait_recv()

    def last_of(block_at):
        if block_at == 0:
            return seg_row[:, tokens - 1 : tokens]
        return seg_before[block_at - 1, 0:1, tokens - 1 : tokens]

    def decay_over(block_at, model, total):
        present = jnp.where(seq > block_at, 1.0, 0.0)
        same = (jnp.abs(last_of(block_at) - last_of(block_at + 1)) < 0.5).astype(jnp.float32)
        return jnp.exp(total) * same * present

    entered = (jnp.abs(seg_col - last_of(1)) < 0.5).astype(jnp.float32) * jnp.where(
        seq > 0, 1.0, 0.0
    )
    for model in (1, 0):
        near_decay = decay_over(0, model, totals[model])
        two = decay_over(1, model, seg_before[0, 1 + model : 2 + model, 0:heads]) * decay_over(
            2, model, seg_before[1, 1 + model : 2 + model, 0:heads]
        )
        for block in blocks:
            decay_own[model : model + 1, block] = widen(
                jnp.broadcast_to(near_decay, (8, heads)), block
            )[0:1, :]
            decay_two[model : model + 1, block] = widen(
                jnp.broadcast_to(two, (8, heads)), block
            )[0:1, :]

    def inside(model):
        run = running[model]
        shifted_t = lax.dot_general(
            shifted[model], eye, (((0,), (0,)), ((), ())), precision=highest
        )
        products[...] = lax.dot_general(
            c_ref[model],
            b_ref[model],
            (((1,), (1,)), ((), ())),
            preferred_element_type=jnp.float32,
        )
        lane = lax.broadcasted_iota(jnp.int32, (1, 128), 1)
        skip = jnp.broadcast_to(skip_ref[model : model + 1, :], (8, heads))
        mid = tokens // 2
        for pair in range(heads // 2):
            columns = pl.ds(128 * pair, 128)
            x_pair = xv[model, :, columns]
            early = late = None
            for q in (0, 1):
                h = 2 * pair + q
                x_one = x_pair * (lane // 64 == q).astype(jnp.bfloat16)
                gap = run[:mid, h : h + 1] - shifted_t[h : h + 1, :mid] + mask[:mid, :mid]
                weights = (jnp.exp(gap) * products[:mid, :mid]).astype(jnp.bfloat16)
                term = jnp.dot(weights, x_one[:mid], preferred_element_type=jnp.float32)
                early = term if early is None else early + term
                gap = run[mid:, h : h + 1] - shifted_t[h : h + 1, :] + mask[mid:, :]
                weights = (jnp.exp(gap) * products[mid:, :]).astype(jnp.bfloat16)
                term = jnp.dot(weights, x_one, preferred_element_type=jnp.float32)
                late = term if late is None else late + term
            passed = x_pair.astype(jnp.float32) * widen(skip, columns)[0:1, :]
            inner[model, :mid, columns] = early + passed[:mid]
            inner[model, mid:, columns] = late + passed[mid:]

    pair_first = copies.take(4)
    pair_copies = {}

    def join_pair(model):
        state_copies[model].wait_recv()
        for block in blocks:
            pair_out[model, :, block] = (
                local_state[model, :, block]
                + decay_own[model : model + 1, block] * state_in[model, :, block].astype(jnp.float32)
            ).astype(jnp.bfloat16)
        pair_copies[model] = [
            start(
                copies.remote(
                    pair_out.at[model],
                    pair_in.at[model, i],
                    pair_first + 2 * model + i,
                    follower(1 + 2 * i),
                )
            )
            for i in (1, 0)
        ]

    def gate(model):
        entry_w = jnp.exp(running[model]) * entered
        squares = jnp.zeros((tokens, 128), jnp.float32)
        for copy in pair_copies[model]:
            copy.wait_recv()
        for block in blocks:
            earlier = pair_in[model, 0, :, block].astype(jnp.float32) + decay_two[
                model : model + 1, block
            ] * pair_in[model, 1, :, block].astype(jnp.float32)
            entering = jnp.dot(
                c_ref[model], earlier.astype(jnp.bfloat16), preferred_element_type=jnp.float32
            )
            ssd_out = inner[model, :, block] + widen(entry_w, block) * entering
            opened = gv[model, :, block].astype(jnp.float32)
            gated = ssd_out * (opened / (1.0 + jnp.exp(-opened)))
            squares = squares + (
                gated[:, :128] * gated[:, :128] + gated[:, 128:] * gated[:, 128:]
            )
            n_ref[model, :, block] = (gated * gain_ref[model : model + 1, block]).astype(
                jnp.bfloat16
            )
        sums_row = lax.dot_general(
            jnp.ones((8, 128), jnp.float32),
            squares,
            (((1,), (1,)), ((), ())),
            precision=highest,
        )
        ss_ref[2 * model : 2 * model + 1, :] = sums_row[0:1, :128]
        ss_ref[2 * model + 1 : 2 * model + 2, :] = sums_row[0:1, 128:]

    inside(1)
    join_pair(1)
    inside(0)
    join_pair(0)
    send_weights(1, (3, 0, 2))
    g_copy.wait()
    ss_ref[...] = jnp.zeros_like(ss_ref)

    token_in = {}
    token_own = {}

    def send_tokens(model):
        at = x
        mine = pl.ds(pl.multiple_of(c * rows, rows), rows)
        theirs = pl.ds(pl.multiple_of(other * rows, rows), rows)
        own = pltpu.make_async_copy(n_ref.at[model, mine], nf.at[model, c, at], local.at[3 + model])
        own.start()
        token_own[model] = own
        first = copies.take(8)
        to_sibling = start(
            copies.remote(n_ref.at[model, theirs], nf.at[model, c, at], first + 4, sibling)
        )
        sends = []
        for core in (0, 1):
            for n, step in ((0, 1), (1, -1)):
                piece = n_ref.at[model, pl.ds(core * rows, rows)]
                copy = pltpu.make_async_remote_copy(
                    src_ref=piece,
                    dst_ref=nf.at[model, c, at],
                    send_sem=send.at[first + 2 * core + n],
                    recv_sem=recv.at[first + 2 * c + n],
                    device_id=token_peer(step, core),
                    device_id_type=MESH,
                )
                sends.append(start(copy))
        token_in[model] = (first, to_sibling)

    def arrival(dst, slot):
        return copies.remote(dst, dst, slot, sibling)

    shared = {}
    onward = {
        1: {1: lower, 3: pl.ds(half // 2, half // 2), 0: pl.ds(0, half // 2)},
        0: {0: upper, 1: lower},
    }

    def forward_weights(model, n):
        at = y
        step, part_rows = order[n][0], order[n][1]
        source = (at - step + size) % size
        arrived[model, n].wait_recv()
        held = wf.at[model, source, c, part_rows]
        if n in onward[model]:
            passed = wf.at[model, source, c, onward[model][n]]
            shared[model, n, "on"] = start(
                copies.remote(passed, passed, copies.take(), weight_peer(step))
            )
        shared[model, n, "near"] = start(copies.remote(held, held, copies.take(), sibling))

    def forward_opposite(model, n):
        source = (y + 2) % size
        shared[model, n, "on"].wait_recv()
        held = wf.at[model, source, c, onward[model][n]]
        shared[model, n, "far"] = start(copies.remote(held, held, copies.take(), sibling))

    token_forward = {}

    def forward_tokens(model):
        at = x
        first, to_sibling = token_in[model]
        forwards = []
        for core, n, step in ((0, 0, 1), (1, 1, -1), (1, 0, 1), (0, 1, -1)):
            source = (at - step + size) % size
            arrival(nf.at[model, core, source], first + 2 * core + n).wait_recv()
            if core == n:
                forwards.append(
                    start(
                        copies.remote(
                            nf.at[model, core, source],
                            nf.at[model, core, source],
                            first + 5 + n,
                            token_peer(step, c),
                        )
                    )
                )
        token_forward[model] = (to_sibling, forwards)

    forward_weights(1, 1)
    gate(1)
    send_tokens(1)
    gate(0)
    forward_weights(1, 3)
    send_weights(0, (1, 3))
    forward_tokens(1)
    send_tokens(0)
    sums_first = copies.take(16)
    sums_local = pltpu.make_async_copy(ss_ref, sums.at[head], local.at[2])
    sums_sent = []
    for i in range(16):
        copy = pltpu.make_async_remote_copy(
            src_ref=ss_ref,
            dst_ref=sums.at[head],
            send_sem=send.at[sums_first + i],
            recv_sem=recv.at[sums_first + head],
            device_id={"seq": (seq + i) % 16, "head": seq},
            device_id_type=MESH,
        )
        sums_sent.append(copy)
        if i == 0:
            pl.when(head != seq)(copy.start)
            pl.when(head == seq)(sums_local.start)
        else:
            copy.start()

    forward_weights(1, 0)
    send_weights(0, (0, 2))
    forward_weights(1, 2)
    forward_opposite(1, 1)

    def piece(model, z_to, e):
        return part.at[model, (2 * (z_to % 2) + e - y + 4) % 4, z_to // 2]

    ring_first = copies.take(112)
    sent_ring = {}
    thin = rows // 4

    def ring_step(model, k, late, own=None):
        e = y % 2 if late else 1 - y % 2
        moves = []
        for v in (0, 1):
            for u, step in ((0, 1), (1, -1)):
                strip = pl.ds((2 * u + v) * thin, thin)
                z_to = (z - step * (1 + k) + 2 * ZS) % ZS
                term = piece(model, z_to, e).at[strip]
                previous, src = None, term
                if k > 0:
                    previous = sent_ring[model, late, u, v, k - 1]
                    src = ring.at[model, late, k - 1, strip]
                copy = copies.remote(
                    src,
                    ring.at[model, late, k, strip],
                    ring_first + 56 * model + 28 * late + 14 * u + 7 * v + k,
                    device(x, y, (z + step + ZS) % ZS, c),
                )
                moves.append((previous, src, term, copy))
                sent_ring[model, late, u, v, k] = copy
                if own is not False:
                    started.append(copy)

        def move():
            for previous, src, term, copy in moves:
                if previous is not None:
                    previous.wait_recv()
                    src[...] = (
                        src[...].astype(jnp.float32) + term[...].astype(jnp.float32)
                    ).astype(src.dtype)
                copy.start()

        if own is None:
            move()
        elif own:
            pl.when((z + 1 + k) % 2 == y // 2)(move)
        else:
            pl.when((z + 1 + k) % 2 != y // 2)(move)

    def multiply(model, j, t):
        total = None
        for core in (0, 1):
            tokens = nf[model, core].reshape(4 * rows, nf.shape[4])
            term = jnp.dot(tokens, wf[model, j, core], preferred_element_type=jnp.float32)
            total = term if total is None else total + term
        part[model, t] = total.reshape(4, rows, total.shape[1]).astype(part.dtype)

    fin_first = copies.take(16)
    finals = []

    def finish(model, late, u):
        e = y % 2 if late else 1 - y % 2
        for v in (0, 1):
            sent_ring[model, late, u, v, 6].wait_recv()
        strip = pl.ds(2 * u * thin, 2 * thin)
        fin_src[model, late, strip] = (
            ring[model, late, 6, strip].astype(jnp.float32)
            + piece(model, z, e)[strip].astype(jnp.float32)
        ).astype(fin_src.dtype)
        src = fin_src.at[model, late, strip]
        dst = fin.at[model, c, strip]
        copy = pltpu.make_async_remote_copy(
            src_ref=src,
            dst_ref=dst,
            send_sem=send.at[fin_first + 8 * model + 2 * late + u],
            recv_sem=recv.at[fin_first + 8 * model + 2 * c + u],
            device_id=device(x, 2 * (z % 2) + e, 2 * (z // 2) + y // 2, y % 2),
            device_id_type=MESH,
        )
        if late:
            here = pltpu.make_async_copy(src, dst, local.at[5 + 2 * model + u])
            pl.when(jnp.logical_not(stays))(copy.start)
            pl.when(stays)(here.start)
            finals.append(copy)
        else:
            start(copy)

    def tokens_ready(model):
        to_sibling, forwards = token_forward[model]
        token_own[model].wait()
        to_sibling.wait_recv()
        for copy in forwards:
            copy.wait_recv()

    def product(model, t):
        at = y
        if t == 0:
            own_local[model].wait()
            forward_later[model].wait_recv()
        elif t == 1:
            shared[model, 1, "near"].wait_recv()
            shared[model, 3, "near"].wait_recv()
        elif t == 3:
            shared[model, 0, "near"].wait_recv()
            shared[model, 2, "near"].wait_recv()
        else:
            for n in onward[model]:
                shared[model, n, "far"].wait_recv()
        multiply(model, (at + t) % 4, t)

    tokens_ready(1)
    product(1, 0)
    product(1, 1)
    product(1, 3)
    ring_step(1, 0, 0)
    forward_opposite(1, 3)
    forward_opposite(1, 0)
    ring_step(1, 1, 0)
    product(1, 2)
    ring_step(1, 0, 1)
    forward_weights(0, 0)
    ring_step(1, 2, 0)
    ring_step(1, 1, 1)
    forward_tokens(0)
    ring_step(1, 3, 0)
    ring_step(1, 2, 1)
    forward_weights(0, 1)
    ring_step(1, 4, 0)
    ring_step(1, 3, 1)
    forward_weights(0, 2)
    tokens_ready(0)
    product(0, 0)
    ring_step(1, 5, 0)
    ring_step(1, 4, 1)
    ring_step(1, 6, 0)
    ring_step(1, 5, 1)
    forward_weights(0, 3)
    product(0, 3)
    ring_step(1, 6, 1)
    product(0, 1)
    ring_step(0, 0, 0)
    for u in (0, 1):
        finish(1, 0, u)
    ring_step(0, 0, 1, True)
    ring_step(0, 1, 0)
    for u in (0, 1):
        finish(1, 1, u)
    forward_opposite(0, 0)
    ring_step(0, 1, 1, True)
    ring_step(0, 2, 0)
    forward_opposite(0, 1)
    ring_step(0, 2, 1, True)
    product(0, 2)
    ring_step(0, 0, 1, False)
    for k in range(3, 7):
        ring_step(0, k, 0)
        ring_step(0, k - 2, 1, False)
        ring_step(0, k, 1, True)
    for u in (0, 1):
        finish(0, 0, u)
    ring_step(0, 5, 1, False)
    ring_step(0, 6, 1, False)

    for i in range(16):
        here = jnp.logical_and(seq == head, head == i)
        arrived = pltpu.make_async_remote_copy(
            src_ref=ss_ref,
            dst_ref=sums.at[i],
            send_sem=send.at[sums_first + i],
            recv_sem=recv.at[sums_first + i],
            device_id=sibling,
            device_id_type=MESH,
        )
        pl.when(here)(sums_local.wait)
        pl.when(jnp.logical_not(here))(arrived.wait_recv)
    mean_square = jnp.sum(sums[...], axis=0) / 16384.0
    scale = lax.rsqrt(mean_square + 1e-05)
    columns = jnp.concatenate([scale] * 16, axis=0).T

    for u in (0, 1):
        finish(0, 1, u)
    for model in (1, 0):
        for core in (0, 1):
            from_self = jnp.logical_and(stays, c == core)
            for u in (0, 1):
                strip = pl.ds(2 * u * thin, 2 * thin)
                dst = fin.at[model, core, strip]
                landed = copies.remote(
                    dst, dst, fin_first + 8 * model + 2 * core + u, sibling
                )
                kept_here = pltpu.make_async_copy(
                    fin_src.at[model, 1, strip], dst, local.at[5 + 2 * model + u]
                )
                pl.when(jnp.logical_not(from_self))(landed.wait_recv)
                pl.when(from_self)(kept_here.wait)
            out_ref[model, core * rows : (core + 1) * rows] = (
                fin[model, core].astype(jnp.float32)
                * columns[:, 2 * model + core : 2 * model + core + 1]
            ).astype(out_ref.dtype)

    for copy in started:
        copy.wait_send()
    for i, copy in enumerate(sums_sent):
        if i == 0:
            pl.when(head != seq)(copy.wait_send)
        else:
            copy.wait_send()
    for copy in finals:
        pl.when(jnp.logical_not(stays))(copy.wait_send)


def local(
    x_heads, gate_z, b_proj, c_proj, dt_raw, dt_bias, decay_rate, skip_d, norm_gain, w_out, seg_ids
):
    tokens, lanes = x_heads.shape[1], x_heads.shape[2]
    depth, width = w_out.shape[1], w_out.shape[2]
    state, rows = b_proj.shape[2], tokens // 2
    bf16, f32 = jnp.bfloat16, jnp.float32
    vmem = pl.BlockSpec(memory_space=pltpu.VMEM)
    hbm = pl.BlockSpec(memory_space=pl.ANY)
    count = 248
    return pl.pallas_call(
        layer_kernel,
        out_shape=jax.ShapeDtypeStruct((2, tokens, width), bf16),
        in_specs=[hbm, hbm] + [vmem] * 8 + [hbm],
        out_specs=vmem,
        scratch_shapes=[
            pltpu.VMEM((2, tokens, lanes), bf16),
            pltpu.VMEM((2, tokens, lanes), bf16),
            pltpu.VMEM((2, tokens, lanes), bf16),
            pltpu.VMEM((8, 128), f32),
            pltpu.VMEM((2, tokens, lanes), f32),
            pltpu.VMEM((tokens, tokens), f32),
            pltpu.VMEM((tokens, tokens), f32),
            pltpu.VMEM((dt_raw.shape[2], lanes), bf16),
            pltpu.VMEM((8, tokens), f32),
            pltpu.VMEM((3, 8, tokens), f32),
            pltpu.VMEM((2, state, lanes), f32),
            pltpu.VMEM((2, state, lanes), bf16),
            pltpu.VMEM((2, state, lanes), bf16),
            pltpu.VMEM((2, state, lanes), bf16),
            pltpu.VMEM((2, 2, state, lanes), bf16),
            pltpu.VMEM((8, lanes), f32),
            pltpu.VMEM((8, lanes), f32),
            pltpu.VMEM((2, 4, 2, depth, width), bf16),
            pltpu.VMEM((2, 2, 4, rows, depth), bf16),
            pltpu.VMEM((2, 4, 4, rows, width), bf16),
            pltpu.VMEM((2, 2, 7, rows, width), bf16),
            pltpu.VMEM((2, 2, rows, width), bf16),
            pltpu.VMEM((2, 2, rows, width), bf16),
            pltpu.VMEM((16, 8, 128), f32),
            pltpu.SemaphoreType.DMA((count,)),
            pltpu.SemaphoreType.DMA((count,)),
            pltpu.SemaphoreType.DMA((11,)),
        ],
        compiler_params=pltpu.CompilerParams(
            collective_id=0, has_side_effects=True, vmem_limit_bytes=62 * 1024 * 1024
        ),
    )(
        x_heads,
        gate_z,
        b_proj,
        c_proj,
        jnp.transpose(dt_raw, (0, 2, 1)),
        dt_bias,
        decay_rate,
        skip_d,
        norm_gain,
        seg_ids.reshape(1, tokens),
        w_out,
    )


def solution(mesh):
    placed = (
        P(None, "seq", "head"),
        P(None, "seq", "head"),
        P(None, "seq", None),
        P(None, "seq", None),
        P(None, "seq", "head"),
        P(None, "head"),
        P(None, "head"),
        P(None, "head"),
        P(None, "head"),
        P(None, "head", "seq"),
        P("seq"),
    )
    return jax.shard_map(
        local, mesh=mesh, in_specs=placed, out_specs=P(None, "head", "seq"), check_vma=False
    )
```

```python
import functools

import jax
import jax.numpy as jnp
from jax import lax
from jax.experimental import pallas as pl
from jax.experimental.pallas import tpu as pltpu
from jax.sharding import PartitionSpec as P

highest = lax.Precision.HIGHEST
FAR = -1e30

MESH = pl.DeviceIdType.MESH
XS, YS, ZS = 4, 4, 8


class Copies:
    def __init__(self, send, recv):
        self.send, self.recv, self.used = send, recv, 0

    def take(self, count=1):
        first = self.used
        self.used += count
        return first

    def remote(self, src, dst, slot, device):
        return pltpu.make_async_remote_copy(
            src_ref=src,
            dst_ref=dst,
            send_sem=self.send.at[slot],
            recv_sem=self.recv.at[slot],
            device_id=device,
            device_id_type=MESH,
        )


def layer_kernel(
    x_hbm, g_hbm, b_ref, c_ref, dt_ref, bias_ref, rate_ref, skip_ref, gain_ref, seg_ref, w_ref,
    out_ref,
    xv, gv, n_ref, ss_ref, inner, mask, products, spread, seg_own, seg_before,
    local_state, state_out, state_in, pair_out, pair_in, decay_own, decay_two,
    wf, nf, part, ring, fin_src, fin, sums, send, recv, local,
):
    seq, head = lax.axis_index("seq"), lax.axis_index("head")
    x, y = seq // YS, seq % YS
    z, c = head // 2, head % 2
    other = 1 - c

    def device(x_at, y_at, z_at, c_at):
        return {"seq": x_at * YS + y_at, "head": z_at * 2 + c_at}

    copies = Copies(send, recv)
    started = []

    def start(copy):
        copy.start()
        started.append(copy)
        return copy

    sibling = device(x, y, z, other)

    def weight_peer(step):
        return device(x, (y + step) % YS, z, c)

    def token_peer(step, core):
        return device((x + step) % XS, y, z, core)

    half = wf.shape[3] // 2
    rows = nf.shape[3]
    tokens, lanes = xv.shape[1], xv.shape[2]
    heads = dt_ref.shape[1]
    upper, lower = pl.ds(0, half), pl.ds(half, half)

    x_copy = pltpu.make_async_copy(x_hbm, xv, local.at[9])
    g_copy = pltpu.make_async_copy(g_hbm, gv, local.at[10])
    x_copy.start()

    def follower(distance):
        return {"seq": (seq + distance) % 16, "head": head}

    barrier = pltpu.get_barrier_semaphore()

    def greet(target):
        pl.semaphore_signal(barrier, inc=1, device_id=target, device_id_type=MESH)

    greet(sibling)
    for step in (1, -1):
        for core in (0, 1):
            greet(device((x + step + XS) % XS, y, z, core))
            greet(device(x, (y + step + YS) % YS, z, core))
        greet(device(x, y, (z + step + ZS) % ZS, c))
    for distance in (1, 2, 3):
        greet(follower(16 - distance))
    stays = jnp.logical_and(z % 2 == y // 2, c == y % 2)
    for core in (0, 1):
        pl.when(jnp.logical_not(jnp.logical_and(stays, c == core)))(
            functools.partial(
                greet, device(x, 2 * (z % 2) + c, 2 * (z // 2) + y // 2, core)
            )
        )
    for i in range(16):
        pl.when(jnp.logical_not(jnp.logical_and(seq == head, head == i)))(
            functools.partial(greet, {"seq": head, "head": i})
        )
    greeted = 32 - stays.astype(jnp.int32) - (seq == head).astype(jnp.int32)

    seg_row = seg_ref[...].astype(jnp.float32)
    seg_own[...] = jnp.broadcast_to(seg_row, seg_own.shape)

    arrived = {}
    size = YS
    own_local = []
    weight_slot = [copies.take(5) for model in (0, 1)]
    order = ((1, upper, 0), (-1, lower, 1), (1, lower, 2), (-1, upper, 3))

    def send_weights(model, which):
        at = y
        for step, part_rows, n in order:
            if n in which:
                copy = start(
                    copies.remote(
                        w_ref.at[model, part_rows],
                        wf.at[model, at, c, part_rows],
                        weight_slot[model] + n,
                        weight_peer(step),
                    )
                )
                arrived[model, n] = copy

    g_copy.start()
    forward_later = {}
    for model in (0, 1):
        at = y
        own = pltpu.make_async_copy(w_ref.at[model], wf.at[model, at, c], local.at[model])
        own.start()
        own_local.append(own)

    def share_own(model):
        forward_later[model] = start(
            copies.remote(
                w_ref.at[model],
                wf.at[model, y, c],
                weight_slot[model] + 4,
                sibling,
            )
        )

    row_at = lax.broadcasted_iota(jnp.int32, (tokens, tokens), 0)
    col_at = lax.broadcasted_iota(jnp.int32, (tokens, tokens), 1)
    eye = (row_at == col_at).astype(jnp.float32)
    lower_ones = (row_at >= col_at).astype(jnp.float32)
    seg_col = lax.dot_general(
        eye, seg_own[...], (((1,), (1,)), ((), ())), precision=highest
    )[:, 0:1]
    mask[...] = jnp.where(
        jnp.logical_and(row_at >= col_at, jnp.abs(seg_col - seg_row) < 0.5), 0.0, FAR
    )
    spread[...] = (
        lax.broadcasted_iota(jnp.int32, spread.shape, 0)
        == lax.broadcasted_iota(jnp.int32, spread.shape, 1) // (lanes // heads)
    ).astype(spread.dtype)
    same_last = (jnp.abs(seg_col - seg_row[:, tokens - 1 : tokens]) < 0.5).astype(jnp.float32)

    def widen(values, columns):
        coarse = values.astype(jnp.bfloat16)
        fine = (values - coarse.astype(jnp.float32)).astype(jnp.bfloat16)
        table = spread[:, columns]
        return jnp.dot(coarse, table, preferred_element_type=jnp.float32) + jnp.dot(
            fine, table, preferred_element_type=jnp.float32
        )

    blocks = [pl.ds(start_at, 256) for start_at in range(0, lanes, 256)]
    state_first = copies.take(2)
    state_copies, running, shifted, totals, tails = {}, {}, {}, {}, {}
    for model in (1, 0):
        raw = (
            lax.dot_general(eye, dt_ref[model], (((1,), (1,)), ((), ())), precision=highest)
            + bias_ref[model : model + 1, :]
        )
        step_size = jnp.maximum(raw, 0.0) + jnp.log1p(jnp.exp(-jnp.abs(raw)))
        log_decay = -(rate_ref[model : model + 1, :] * step_size)
        run = jnp.dot(lower_ones, log_decay, precision=highest)
        total = run[tokens - 1 : tokens, :]
        tails[model] = jnp.exp(total - run) * same_last * step_size
        running[model] = run
        totals[model] = total
        shifted[model] = run - jnp.log(step_size)
        seg_own[1 + model : 2 + model, 0:heads] = total

    def own_state(model):
        for block in blocks:
            weighted = (
                xv[model, :, block].astype(jnp.float32) * widen(tails[model], block)
            ).astype(jnp.bfloat16)
            fresh = lax.dot_general(
                b_ref[model],
                weighted,
                (((0,), (0,)), ((), ())),
                preferred_element_type=jnp.float32,
            )
            local_state[model, :, block] = fresh
            state_out[model, :, block] = fresh.astype(jnp.bfloat16)

    def send_state(model):
        state_copies[model] = start(
            copies.remote(
                state_out.at[model], state_in.at[model], state_first + model, follower(1)
            )
        )

    x_copy.wait()
    own_state(1)
    pl.semaphore_wait(barrier, greeted)
    info_first = copies.take(3)
    info_copies = [
        start(copies.remote(seg_own, seg_before.at[i], info_first + i, follower(i + 1)))
        for i in range(3)
    ]
    send_state(1)
    send_weights(1, (1,))
    own_state(0)
    send_state(0)
    share_own(1)
    share_own(0)

    for copy in info_copies:
        copy.wait_recv()

    def last_of(block_at):
        if block_at == 0:
            return seg_row[:, tokens - 1 : tokens]
        return seg_before[block_at - 1, 0:1, tokens - 1 : tokens]

    def decay_over(block_at, model, total):
        present = jnp.where(seq > block_at, 1.0, 0.0)
        same = (jnp.abs(last_of(block_at) - last_of(block_at + 1)) < 0.5).astype(jnp.float32)
        return jnp.exp(total) * same * present

    entered = (jnp.abs(seg_col - last_of(1)) < 0.5).astype(jnp.float32) * jnp.where(
        seq > 0, 1.0, 0.0
    )
    for model in (1, 0):
        near_decay = decay_over(0, model, totals[model])
        two = decay_over(1, model, seg_before[0, 1 + model : 2 + model, 0:heads]) * decay_over(
            2, model, seg_before[1, 1 + model : 2 + model, 0:heads]
        )
        for block in blocks:
            decay_own[model : model + 1, block] = widen(
                jnp.broadcast_to(near_decay, (8, heads)), block
            )[0:1, :]
            decay_two[model : model + 1, block] = widen(
                jnp.broadcast_to(two, (8, heads)), block
            )[0:1, :]

    def inside(model):
        run = running[model]
        shifted_t = lax.dot_general(
            shifted[model], eye, (((0,), (0,)), ((), ())), precision=highest
        )
        products[...] = lax.dot_general(
            c_ref[model],
            b_ref[model],
            (((1,), (1,)), ((), ())),
            preferred_element_type=jnp.float32,
        )
        lane = lax.broadcasted_iota(jnp.int32, (1, 128), 1)
        skip = jnp.broadcast_to(skip_ref[model : model + 1, :], (8, heads))
        mid = tokens // 2
        for pair in range(heads // 2):
            columns = pl.ds(128 * pair, 128)
            x_pair = xv[model, :, columns]
            early = late = None
            for q in (0, 1):
                h = 2 * pair + q
                x_one = x_pair * (lane // 64 == q).astype(jnp.bfloat16)
                gap = run[:mid, h : h + 1] - shifted_t[h : h + 1, :mid] + mask[:mid, :mid]
                weights = (jnp.exp(gap) * products[:mid, :mid]).astype(jnp.bfloat16)
                term = jnp.dot(weights, x_one[:mid], preferred_element_type=jnp.float32)
                early = term if early is None else early + term
                gap = run[mid:, h : h + 1] - shifted_t[h : h + 1, :] + mask[mid:, :]
                weights = (jnp.exp(gap) * products[mid:, :]).astype(jnp.bfloat16)
                term = jnp.dot(weights, x_one, preferred_element_type=jnp.float32)
                late = term if late is None else late + term
            passed = x_pair.astype(jnp.float32) * widen(skip, columns)[0:1, :]
            inner[model, :mid, columns] = early + passed[:mid]
            inner[model, mid:, columns] = late + passed[mid:]

    pair_first = copies.take(4)
    pair_copies = {}

    def join_pair(model):
        state_copies[model].wait_recv()
        for block in blocks:
            pair_out[model, :, block] = (
                local_state[model, :, block]
                + decay_own[model : model + 1, block] * state_in[model, :, block].astype(jnp.float32)
            ).astype(jnp.bfloat16)
        pair_copies[model] = [
            start(
                copies.remote(
                    pair_out.at[model],
                    pair_in.at[model, i],
                    pair_first + 2 * model + i,
                    follower(1 + 2 * i),
                )
            )
            for i in (1, 0)
        ]

    def gate(model):
        entry_w = jnp.exp(running[model]) * entered
        squares = jnp.zeros((tokens, 128), jnp.float32)
        for copy in pair_copies[model]:
            copy.wait_recv()
        for block in blocks:
            earlier = pair_in[model, 0, :, block].astype(jnp.float32) + decay_two[
                model : model + 1, block
            ] * pair_in[model, 1, :, block].astype(jnp.float32)
            entering = jnp.dot(
                c_ref[model], earlier.astype(jnp.bfloat16), preferred_element_type=jnp.float32
            )
            ssd_out = inner[model, :, block] + widen(entry_w, block) * entering
            opened = gv[model, :, block].astype(jnp.float32)
            gated = ssd_out * (opened / (1.0 + jnp.exp(-opened)))
            squares = squares + (
                gated[:, :128] * gated[:, :128] + gated[:, 128:] * gated[:, 128:]
            )
            n_ref[model, :, block] = (gated * gain_ref[model : model + 1, block]).astype(
                jnp.bfloat16
            )
        sums_row = lax.dot_general(
            jnp.ones((8, 128), jnp.float32),
            squares,
            (((1,), (1,)), ((), ())),
            precision=highest,
        )
        ss_ref[2 * model : 2 * model + 1, :] = sums_row[0:1, :128]
        ss_ref[2 * model + 1 : 2 * model + 2, :] = sums_row[0:1, 128:]

    inside(1)
    join_pair(1)
    inside(0)
    join_pair(0)
    send_weights(1, (3, 0, 2))
    g_copy.wait()
    ss_ref[...] = jnp.zeros_like(ss_ref)

    token_in = {}
    token_own = {}

    def send_tokens(model):
        at = x
        mine = pl.ds(pl.multiple_of(c * rows, rows), rows)
        theirs = pl.ds(pl.multiple_of(other * rows, rows), rows)
        own = pltpu.make_async_copy(n_ref.at[model, mine], nf.at[model, c, at], local.at[3 + model])
        own.start()
        token_own[model] = own
        first = copies.take(8)
        to_sibling = start(
            copies.remote(n_ref.at[model, theirs], nf.at[model, c, at], first + 4, sibling)
        )
        sends = []
        for core in (0, 1):
            for n, step in ((0, 1), (1, -1)):
                piece = n_ref.at[model, pl.ds(core * rows, rows)]
                copy = pltpu.make_async_remote_copy(
                    src_ref=piece,
                    dst_ref=nf.at[model, c, at],
                    send_sem=send.at[first + 2 * core + n],
                    recv_sem=recv.at[first + 2 * c + n],
                    device_id=token_peer(step, core),
                    device_id_type=MESH,
                )
                sends.append(start(copy))
        token_in[model] = (first, to_sibling)

    def arrival(dst, slot):
        return copies.remote(dst, dst, slot, sibling)

    shared = {}
    onward = {
        1: {1: lower, 3: pl.ds(half // 2, half // 2), 0: pl.ds(0, half // 2)},
        0: {0: upper, 1: lower},
    }

    def forward_weights(model, n):
        at = y
        step, part_rows = order[n][0], order[n][1]
        source = (at - step + size) % size
        arrived[model, n].wait_recv()
        held = wf.at[model, source, c, part_rows]
        if n in onward[model]:
            passed = wf.at[model, source, c, onward[model][n]]
            shared[model, n, "on"] = start(
                copies.remote(passed, passed, copies.take(), weight_peer(step))
            )
        shared[model, n, "near"] = start(copies.remote(held, held, copies.take(), sibling))

    def forward_opposite(model, n):
        source = (y + 2) % size
        shared[model, n, "on"].wait_recv()
        held = wf.at[model, source, c, onward[model][n]]
        shared[model, n, "far"] = start(copies.remote(held, held, copies.take(), sibling))

    token_forward = {}

    def forward_tokens(model):
        at = x
        first, to_sibling = token_in[model]
        forwards = []
        for core, n, step in ((0, 0, 1), (1, 1, -1), (1, 0, 1), (0, 1, -1)):
            source = (at - step + size) % size
            arrival(nf.at[model, core, source], first + 2 * core + n).wait_recv()
            if core == n:
                forwards.append(
                    start(
                        copies.remote(
                            nf.at[model, core, source],
                            nf.at[model, core, source],
                            first + 5 + n,
                            token_peer(step, c),
                        )
                    )
                )
        token_forward[model] = (to_sibling, forwards)

    forward_weights(1, 1)
    gate(1)
    send_tokens(1)
    gate(0)
    forward_weights(1, 3)
    send_weights(0, (1, 3))
    forward_tokens(1)
    send_tokens(0)
    sums_first = copies.take(16)
    sums_local = pltpu.make_async_copy(ss_ref, sums.at[head], local.at[2])
    sums_sent = []
    for i in range(16):
        copy = pltpu.make_async_remote_copy(
            src_ref=ss_ref,
            dst_ref=sums.at[head],
            send_sem=send.at[sums_first + i],
            recv_sem=recv.at[sums_first + head],
            device_id={"seq": (seq + i) % 16, "head": seq},
            device_id_type=MESH,
        )
        sums_sent.append(copy)
        if i == 0:
            pl.when(head != seq)(copy.start)
            pl.when(head == seq)(sums_local.start)
        else:
            copy.start()

    forward_weights(1, 0)
    send_weights(0, (0, 2))
    forward_weights(1, 2)
    forward_opposite(1, 1)

    def piece(model, z_to, e):
        return part.at[model, (2 * (z_to % 2) + e - y + 4) % 4, z_to // 2]

    ring_first = copies.take(112)
    sent_ring = {}
    thin = rows // 4

    def ring_step(model, k, late, own=None):
        e = y % 2 if late else 1 - y % 2
        moves = []
        for v in (0, 1):
            for u, step in ((0, 1), (1, -1)):
                strip = pl.ds((2 * u + v) * thin, thin)
                z_to = (z - step * (1 + k) + 2 * ZS) % ZS
                term = piece(model, z_to, e).at[strip]
                previous, src = None, term
                if k > 0:
                    previous = sent_ring[model, late, u, v, k - 1]
                    src = ring.at[model, late, k - 1, strip]
                copy = copies.remote(
                    src,
                    ring.at[model, late, k, strip],
                    ring_first + 56 * model + 28 * late + 14 * u + 7 * v + k,
                    device(x, y, (z + step + ZS) % ZS, c),
                )
                moves.append((previous, src, term, copy))
                sent_ring[model, late, u, v, k] = copy
                if own is not False:
                    started.append(copy)

        def move():
            for previous, src, term, copy in moves:
                if previous is not None:
                    previous.wait_recv()
                    src[...] = (
                        src[...].astype(jnp.float32) + term[...].astype(jnp.float32)
                    ).astype(src.dtype)
                copy.start()

        if own is None:
            move()
        elif own:
            pl.when((z + 1 + k) % 2 == y // 2)(move)
        else:
            pl.when((z + 1 + k) % 2 != y // 2)(move)

    def multiply(model, j, t):
        total = None
        for core in (0, 1):
            tokens = nf[model, core].reshape(4 * rows, nf.shape[4])
            term = jnp.dot(tokens, wf[model, j, core], preferred_element_type=jnp.float32)
            total = term if total is None else total + term
        part[model, t] = total.reshape(4, rows, total.shape[1]).astype(part.dtype)

    fin_first = copies.take(16)
    finals = []

    def finish(model, late, u):
        e = y % 2 if late else 1 - y % 2
        for v in (0, 1):
            sent_ring[model, late, u, v, 6].wait_recv()
        strip = pl.ds(2 * u * thin, 2 * thin)
        fin_src[model, late, strip] = (
            ring[model, late, 6, strip].astype(jnp.float32)
            + piece(model, z, e)[strip].astype(jnp.float32)
        ).astype(fin_src.dtype)
        src = fin_src.at[model, late, strip]
        dst = fin.at[model, c, strip]
        copy = pltpu.make_async_remote_copy(
            src_ref=src,
            dst_ref=dst,
            send_sem=send.at[fin_first + 8 * model + 2 * late + u],
            recv_sem=recv.at[fin_first + 8 * model + 2 * c + u],
            device_id=device(x, 2 * (z % 2) + e, 2 * (z // 2) + y // 2, y % 2),
            device_id_type=MESH,
        )
        if late:
            here = pltpu.make_async_copy(src, dst, local.at[5 + 2 * model + u])
            pl.when(jnp.logical_not(stays))(copy.start)
            pl.when(stays)(here.start)
            finals.append(copy)
        else:
            start(copy)

    def tokens_ready(model):
        to_sibling, forwards = token_forward[model]
        token_own[model].wait()
        to_sibling.wait_recv()
        for copy in forwards:
            copy.wait_recv()

    def product(model, t):
        at = y
        if t == 0:
            own_local[model].wait()
            forward_later[model].wait_recv()
        elif t == 1:
            shared[model, 1, "near"].wait_recv()
            shared[model, 3, "near"].wait_recv()
        elif t == 3:
            shared[model, 0, "near"].wait_recv()
            shared[model, 2, "near"].wait_recv()
        else:
            for n in onward[model]:
                shared[model, n, "far"].wait_recv()
        multiply(model, (at + t) % 4, t)

    tokens_ready(1)
    product(1, 0)
    product(1, 1)
    product(1, 3)
    ring_step(1, 0, 0)
    forward_opposite(1, 3)
    forward_opposite(1, 0)
    ring_step(1, 1, 0)
    product(1, 2)
    ring_step(1, 0, 1)
    ring_step(1, 2, 0)
    ring_step(1, 1, 1)
    forward_tokens(0)
    ring_step(1, 3, 0)
    ring_step(1, 2, 1)
    forward_weights(0, 0)
    ring_step(1, 4, 0)
    ring_step(1, 3, 1)
    forward_weights(0, 1)
    ring_step(1, 5, 0)
    ring_step(1, 4, 1)
    forward_weights(0, 2)
    tokens_ready(0)
    product(0, 0)
    ring_step(1, 6, 0)
    ring_step(1, 5, 1)
    forward_weights(0, 3)
    product(0, 3)
    ring_step(1, 6, 1)
    product(0, 1)
    ring_step(0, 0, 0)
    ring_step(0, 0, 1, True)
    forward_opposite(0, 0)
    ring_step(0, 1, 0)
    ring_step(0, 1, 1, True)
    for u in (0, 1):
        finish(1, 0, u)
    forward_opposite(0, 1)
    ring_step(0, 2, 0)
    product(0, 2)
    ring_step(0, 0, 1, False)
    ring_step(0, 2, 1, True)
    ring_step(0, 1, 1, False)
    for u in (0, 1):
        finish(1, 1, u)
    for k in range(3, 7):
        ring_step(0, k, 0)
        ring_step(0, k - 1, 1, False)
        ring_step(0, k, 1, True)
    for u in (0, 1):
        finish(0, 0, u)
    ring_step(0, 6, 1, False)

    for i in range(16):
        here = jnp.logical_and(seq == head, head == i)
        arrived = pltpu.make_async_remote_copy(
            src_ref=ss_ref,
            dst_ref=sums.at[i],
            send_sem=send.at[sums_first + i],
            recv_sem=recv.at[sums_first + i],
            device_id=sibling,
            device_id_type=MESH,
        )
        pl.when(here)(sums_local.wait)
        pl.when(jnp.logical_not(here))(arrived.wait_recv)
    mean_square = jnp.sum(sums[...], axis=0) / 16384.0
    scale = lax.rsqrt(mean_square + 1e-05)
    columns = jnp.concatenate([scale] * 16, axis=0).T

    for u in (0, 1):
        finish(0, 1, u)
    for model in (1, 0):
        for core in (0, 1):
            from_self = jnp.logical_and(stays, c == core)
            for u in (0, 1):
                strip = pl.ds(2 * u * thin, 2 * thin)
                dst = fin.at[model, core, strip]
                landed = copies.remote(
                    dst, dst, fin_first + 8 * model + 2 * core + u, sibling
                )
                kept_here = pltpu.make_async_copy(
                    fin_src.at[model, 1, strip], dst, local.at[5 + 2 * model + u]
                )
                pl.when(jnp.logical_not(from_self))(landed.wait_recv)
                pl.when(from_self)(kept_here.wait)
            out_ref[model, core * rows : (core + 1) * rows] = (
                fin[model, core].astype(jnp.float32)
                * columns[:, 2 * model + core : 2 * model + core + 1]
            ).astype(out_ref.dtype)

    for copy in started:
        copy.wait_send()
    for i, copy in enumerate(sums_sent):
        if i == 0:
            pl.when(head != seq)(copy.wait_send)
        else:
            copy.wait_send()
    for copy in finals:
        pl.when(jnp.logical_not(stays))(copy.wait_send)


def local(
    x_heads, gate_z, b_proj, c_proj, dt_raw, dt_bias, decay_rate, skip_d, norm_gain, w_out, seg_ids
):
    tokens, lanes = x_heads.shape[1], x_heads.shape[2]
    depth, width = w_out.shape[1], w_out.shape[2]
    state, rows = b_proj.shape[2], tokens // 2
    bf16, f32 = jnp.bfloat16, jnp.float32
    vmem = pl.BlockSpec(memory_space=pltpu.VMEM)
    hbm = pl.BlockSpec(memory_space=pl.ANY)
    count = 248
    return pl.pallas_call(
        layer_kernel,
        out_shape=jax.ShapeDtypeStruct((2, tokens, width), bf16),
        in_specs=[hbm, hbm] + [vmem] * 8 + [hbm],
        out_specs=vmem,
        scratch_shapes=[
            pltpu.VMEM((2, tokens, lanes), bf16),
            pltpu.VMEM((2, tokens, lanes), bf16),
            pltpu.VMEM((2, tokens, lanes), bf16),
            pltpu.VMEM((8, 128), f32),
            pltpu.VMEM((2, tokens, lanes), f32),
            pltpu.VMEM((tokens, tokens), f32),
            pltpu.VMEM((tokens, tokens), f32),
            pltpu.VMEM((dt_raw.shape[2], lanes), bf16),
            pltpu.VMEM((8, tokens), f32),
            pltpu.VMEM((3, 8, tokens), f32),
            pltpu.VMEM((2, state, lanes), f32),
            pltpu.VMEM((2, state, lanes), bf16),
            pltpu.VMEM((2, state, lanes), bf16),
            pltpu.VMEM((2, state, lanes), bf16),
            pltpu.VMEM((2, 2, state, lanes), bf16),
            pltpu.VMEM((8, lanes), f32),
            pltpu.VMEM((8, lanes), f32),
            pltpu.VMEM((2, 4, 2, depth, width), bf16),
            pltpu.VMEM((2, 2, 4, rows, depth), bf16),
            pltpu.VMEM((2, 4, 4, rows, width), bf16),
            pltpu.VMEM((2, 2, 7, rows, width), bf16),
            pltpu.VMEM((2, 2, rows, width), bf16),
            pltpu.VMEM((2, 2, rows, width), bf16),
            pltpu.VMEM((16, 8, 128), f32),
            pltpu.SemaphoreType.DMA((count,)),
            pltpu.SemaphoreType.DMA((count,)),
            pltpu.SemaphoreType.DMA((11,)),
        ],
        compiler_params=pltpu.CompilerParams(
            collective_id=0, has_side_effects=True, vmem_limit_bytes=62 * 1024 * 1024
        ),
    )(
        x_heads,
        gate_z,
        b_proj,
        c_proj,
        jnp.transpose(dt_raw, (0, 2, 1)),
        dt_bias,
        decay_rate,
        skip_d,
        norm_gain,
        seg_ids.reshape(1, tokens),
        w_out,
    )


def solution(mesh):
    placed = (
        P(None, "seq", "head"),
        P(None, "seq", "head"),
        P(None, "seq", None),
        P(None, "seq", None),
        P(None, "seq", "head"),
        P(None, "head"),
        P(None, "head"),
        P(None, "head"),
        P(None, "head"),
        P(None, "head", "seq"),
        P("seq"),
    )
    return jax.shard_map(
        local, mesh=mesh, in_specs=placed, out_specs=P(None, "head", "seq"), check_vma=False
    )
```

```python
import functools

import jax
import jax.numpy as jnp
from jax import lax
from jax.experimental import pallas as pl
from jax.experimental.pallas import tpu as pltpu
from jax.sharding import PartitionSpec as P

highest = lax.Precision.HIGHEST
FAR = -1e30
RING_AT = 85

MESH = pl.DeviceIdType.MESH
XS, YS, ZS = 4, 4, 8


class Copies:
    def __init__(self, send, recv):
        self.send, self.recv, self.used, self.sends = send, recv, 0, 0

    def take(self, count=1, sends=None):
        first = self.used
        self.used += count
        self.sends += count if sends is None else sends
        return first

    def remote(self, src, dst, slot, device, send_slot=None):
        return pltpu.make_async_remote_copy(
            src_ref=src,
            dst_ref=dst,
            send_sem=self.send.at[slot if send_slot is None else send_slot],
            recv_sem=self.recv.at[slot],
            device_id=device,
            device_id_type=MESH,
        )


def layer_kernel(
    x_hbm, g_hbm, b_ref, c_ref, dt_ref, bias_ref, rate_ref, skip_ref, gain_ref, seg_ref, w_ref,
    out_ref,
    xv, gv, n_ref, ss_ref, inner, mask, products, spread, seg_own, seg_before,
    local_state, state_out, state_in, pair_out, pair_in, decay_own, decay_two,
    wf, nf, part, ring, fin_src, fin, sums, send, recv, local,
):
    seq, head = lax.axis_index("seq"), lax.axis_index("head")
    x, y = seq // YS, seq % YS
    z, c = head // 2, head % 2
    other = 1 - c

    def device(x_at, y_at, z_at, c_at):
        return {"seq": x_at * YS + y_at, "head": z_at * 2 + c_at}

    copies = Copies(send, recv)
    started = []

    def start(copy):
        copy.start()
        started.append(copy)
        return copy

    sibling = device(x, y, z, other)

    def weight_peer(step):
        return device(x, (y + step) % YS, z, c)

    def token_peer(step, core):
        return device((x + step) % XS, y, z, core)

    half = wf.shape[3] // 2
    rows = nf.shape[3]
    tokens, lanes = xv.shape[1], xv.shape[2]
    heads = dt_ref.shape[1]
    upper, lower = pl.ds(0, half), pl.ds(half, half)

    x_copy = pltpu.make_async_copy(x_hbm, xv, local.at[9])
    g_copy = pltpu.make_async_copy(g_hbm, gv, local.at[10])
    x_copy.start()

    def follower(distance):
        return {"seq": (seq + distance) % 16, "head": head}

    barrier = pltpu.get_barrier_semaphore()

    def greet(target):
        pl.semaphore_signal(barrier, inc=1, device_id=target, device_id_type=MESH)

    greet(sibling)
    for step in (1, -1):
        for core in (0, 1):
            greet(device((x + step + XS) % XS, y, z, core))
            greet(device(x, (y + step + YS) % YS, z, core))
        greet(device(x, y, (z + step + ZS) % ZS, c))
    for distance in (1, 2, 3):
        greet(follower(16 - distance))
    stays = jnp.logical_and(z % 2 == y // 2, c == y % 2)
    for core in (0, 1):
        pl.when(jnp.logical_not(jnp.logical_and(stays, c == core)))(
            functools.partial(
                greet, device(x, 2 * (z % 2) + c, 2 * (z // 2) + y // 2, core)
            )
        )
    for i in range(16):
        pl.when(jnp.logical_not(jnp.logical_and(seq == head, head == i)))(
            functools.partial(greet, {"seq": head, "head": i})
        )
    greeted = 32 - stays.astype(jnp.int32) - (seq == head).astype(jnp.int32)

    seg_row = seg_ref[...].astype(jnp.float32)
    seg_own[...] = jnp.broadcast_to(seg_row, seg_own.shape)

    arrived = {}
    size = YS
    own_local = []
    weight_slot = [copies.take(5) for model in (0, 1)]
    order = ((1, upper, 0), (-1, lower, 1), (1, lower, 2), (-1, upper, 3))

    def send_weights(model, which):
        at = y
        for step, part_rows, n in order:
            if n in which:
                copy = start(
                    copies.remote(
                        w_ref.at[model, part_rows],
                        wf.at[model, at, c, part_rows],
                        weight_slot[model] + n,
                        weight_peer(step),
                    )
                )
                arrived[model, n] = copy

    g_copy.start()
    forward_later = {}
    for model in (0, 1):
        at = y
        own = pltpu.make_async_copy(w_ref.at[model], wf.at[model, at, c], local.at[model])
        own.start()
        own_local.append(own)

    def share_own(model):
        forward_later[model] = start(
            copies.remote(
                w_ref.at[model],
                wf.at[model, y, c],
                weight_slot[model] + 4,
                sibling,
            )
        )

    row_at = lax.broadcasted_iota(jnp.int32, (tokens, tokens), 0)
    col_at = lax.broadcasted_iota(jnp.int32, (tokens, tokens), 1)
    eye = (row_at == col_at).astype(jnp.float32)
    lower_ones = (row_at >= col_at).astype(jnp.float32)
    seg_col = lax.dot_general(
        eye, seg_own[...], (((1,), (1,)), ((), ())), precision=highest
    )[:, 0:1]
    mask[...] = jnp.where(
        jnp.logical_and(row_at >= col_at, jnp.abs(seg_col - seg_row) < 0.5), 0.0, FAR
    )
    spread[...] = (
        lax.broadcasted_iota(jnp.int32, spread.shape, 0)
        == lax.broadcasted_iota(jnp.int32, spread.shape, 1) // (lanes // heads)
    ).astype(spread.dtype)
    same_last = (jnp.abs(seg_col - seg_row[:, tokens - 1 : tokens]) < 0.5).astype(jnp.float32)

    def widen(values, columns):
        coarse = values.astype(jnp.bfloat16)
        fine = (values - coarse.astype(jnp.float32)).astype(jnp.bfloat16)
        table = spread[:, columns]
        return jnp.dot(coarse, table, preferred_element_type=jnp.float32) + jnp.dot(
            fine, table, preferred_element_type=jnp.float32
        )

    blocks = [pl.ds(start_at, 256) for start_at in range(0, lanes, 256)]
    state_first = copies.take(2)
    state_copies, running, shifted, totals, tails = {}, {}, {}, {}, {}
    for model in (1, 0):
        raw = (
            lax.dot_general(eye, dt_ref[model], (((1,), (1,)), ((), ())), precision=highest)
            + bias_ref[model : model + 1, :]
        )
        step_size = jnp.maximum(raw, 0.0) + jnp.log1p(jnp.exp(-jnp.abs(raw)))
        log_decay = -(rate_ref[model : model + 1, :] * step_size)
        run = jnp.dot(lower_ones, log_decay, precision=highest)
        total = run[tokens - 1 : tokens, :]
        tails[model] = jnp.exp(total - run) * same_last * step_size
        running[model] = run
        totals[model] = total
        shifted[model] = run - jnp.log(step_size)
        seg_own[1 + model : 2 + model, 0:heads] = total

    def own_state(model):
        for block in blocks:
            weighted = (
                xv[model, :, block].astype(jnp.float32) * widen(tails[model], block)
            ).astype(jnp.bfloat16)
            fresh = lax.dot_general(
                b_ref[model],
                weighted,
                (((0,), (0,)), ((), ())),
                preferred_element_type=jnp.float32,
            )
            local_state[model, :, block] = fresh
            state_out[model, :, block] = fresh.astype(jnp.bfloat16)

    def send_state(model):
        state_copies[model] = start(
            copies.remote(
                state_out.at[model], state_in.at[model], state_first + model, follower(1)
            )
        )

    x_copy.wait()
    own_state(1)
    pl.semaphore_wait(barrier, greeted)
    info_first = copies.take(3)
    info_copies = [
        start(copies.remote(seg_own, seg_before.at[i], info_first + i, follower(i + 1)))
        for i in range(3)
    ]
    send_state(1)
    send_weights(1, (1,))
    own_state(0)
    send_state(0)
    share_own(1)
    share_own(0)

    for copy in info_copies:
        copy.wait_recv()

    def last_of(block_at):
        if block_at == 0:
            return seg_row[:, tokens - 1 : tokens]
        return seg_before[block_at - 1, 0:1, tokens - 1 : tokens]

    def decay_over(block_at, model, total):
        present = jnp.where(seq > block_at, 1.0, 0.0)
        same = (jnp.abs(last_of(block_at) - last_of(block_at + 1)) < 0.5).astype(jnp.float32)
        return jnp.exp(total) * same * present

    entered = (jnp.abs(seg_col - last_of(1)) < 0.5).astype(jnp.float32) * jnp.where(
        seq > 0, 1.0, 0.0
    )
    for model in (1, 0):
        near_decay = decay_over(0, model, totals[model])
        two = decay_over(1, model, seg_before[0, 1 + model : 2 + model, 0:heads]) * decay_over(
            2, model, seg_before[1, 1 + model : 2 + model, 0:heads]
        )
        for block in blocks:
            decay_own[model : model + 1, block] = widen(
                jnp.broadcast_to(near_decay, (8, heads)), block
            )[0:1, :]
            decay_two[model : model + 1, block] = widen(
                jnp.broadcast_to(two, (8, heads)), block
            )[0:1, :]

    def inside(model):
        run = running[model]
        shifted_t = lax.dot_general(
            shifted[model], eye, (((0,), (0,)), ((), ())), precision=highest
        )
        products[...] = lax.dot_general(
            c_ref[model],
            b_ref[model],
            (((1,), (1,)), ((), ())),
            preferred_element_type=jnp.float32,
        )
        lane = lax.broadcasted_iota(jnp.int32, (1, 128), 1)
        skip = jnp.broadcast_to(skip_ref[model : model + 1, :], (8, heads))
        mid = tokens // 2
        for pair in range(heads // 2):
            columns = pl.ds(128 * pair, 128)
            x_pair = xv[model, :, columns]
            early = late = None
            for q in (0, 1):
                h = 2 * pair + q
                x_one = x_pair * (lane // 64 == q).astype(jnp.bfloat16)
                gap = run[:mid, h : h + 1] - shifted_t[h : h + 1, :mid] + mask[:mid, :mid]
                weights = (jnp.exp(gap) * products[:mid, :mid]).astype(jnp.bfloat16)
                term = jnp.dot(weights, x_one[:mid], preferred_element_type=jnp.float32)
                early = term if early is None else early + term
                gap = run[mid:, h : h + 1] - shifted_t[h : h + 1, :] + mask[mid:, :]
                weights = (jnp.exp(gap) * products[mid:, :]).astype(jnp.bfloat16)
                term = jnp.dot(weights, x_one, preferred_element_type=jnp.float32)
                late = term if late is None else late + term
            passed = x_pair.astype(jnp.float32) * widen(skip, columns)[0:1, :]
            inner[model, :mid, columns] = early + passed[:mid]
            inner[model, mid:, columns] = late + passed[mid:]

    pair_first = copies.take(4)
    pair_copies = {}

    def join_pair(model):
        state_copies[model].wait_recv()
        for block in blocks:
            pair_out[model, :, block] = (
                local_state[model, :, block]
                + decay_own[model : model + 1, block] * state_in[model, :, block].astype(jnp.float32)
            ).astype(jnp.bfloat16)
        pair_copies[model] = [
            start(
                copies.remote(
                    pair_out.at[model],
                    pair_in.at[model, i],
                    pair_first + 2 * model + i,
                    follower(1 + 2 * i),
                )
            )
            for i in (1, 0)
        ]

    def gate(model):
        entry_w = jnp.exp(running[model]) * entered
        squares = jnp.zeros((tokens, 128), jnp.float32)
        for copy in pair_copies[model]:
            copy.wait_recv()
        for block in blocks:
            earlier = pair_in[model, 0, :, block].astype(jnp.float32) + decay_two[
                model : model + 1, block
            ] * pair_in[model, 1, :, block].astype(jnp.float32)
            entering = jnp.dot(
                c_ref[model], earlier.astype(jnp.bfloat16), preferred_element_type=jnp.float32
            )
            ssd_out = inner[model, :, block] + widen(entry_w, block) * entering
            opened = gv[model, :, block].astype(jnp.float32)
            gated = ssd_out * (opened / (1.0 + jnp.exp(-opened)))
            squares = squares + (
                gated[:, :128] * gated[:, :128] + gated[:, 128:] * gated[:, 128:]
            )
            n_ref[model, :, block] = (gated * gain_ref[model : model + 1, block]).astype(
                jnp.bfloat16
            )
        sums_row = lax.dot_general(
            jnp.ones((8, 128), jnp.float32),
            squares,
            (((1,), (1,)), ((), ())),
            precision=highest,
        )
        ss_ref[2 * model : 2 * model + 1, :] = sums_row[0:1, :128]
        ss_ref[2 * model + 1 : 2 * model + 2, :] = sums_row[0:1, 128:]

    inside(1)
    join_pair(1)
    inside(0)
    join_pair(0)
    send_weights(1, (3, 0, 2))
    g_copy.wait()
    ss_ref[...] = jnp.zeros_like(ss_ref)

    token_in = {}
    token_own = {}

    def send_tokens(model):
        at = x
        mine = pl.ds(pl.multiple_of(c * rows, rows), rows)
        theirs = pl.ds(pl.multiple_of(other * rows, rows), rows)
        own = pltpu.make_async_copy(n_ref.at[model, mine], nf.at[model, c, at], local.at[3 + model])
        own.start()
        token_own[model] = own
        first = copies.take(8)
        to_sibling = start(
            copies.remote(n_ref.at[model, theirs], nf.at[model, c, at], first + 4, sibling)
        )
        sends = []
        for core in (0, 1):
            for n, step in ((0, 1), (1, -1)):
                piece = n_ref.at[model, pl.ds(core * rows, rows)]
                copy = pltpu.make_async_remote_copy(
                    src_ref=piece,
                    dst_ref=nf.at[model, c, at],
                    send_sem=send.at[first + 2 * core + n],
                    recv_sem=recv.at[first + 2 * c + n],
                    device_id=token_peer(step, core),
                    device_id_type=MESH,
                )
                sends.append(start(copy))
        token_in[model] = (first, to_sibling)

    def arrival(dst, slot):
        return copies.remote(dst, dst, slot, sibling)

    shared = {}
    onward = {
        1: {1: lower, 3: pl.ds(half // 2, half // 2), 0: pl.ds(0, half // 2)},
        0: {0: upper, 1: lower},
    }

    def forward_weights(model, n):
        at = y
        step, part_rows = order[n][0], order[n][1]
        source = (at - step + size) % size
        arrived[model, n].wait_recv()
        held = wf.at[model, source, c, part_rows]
        if n in onward[model]:
            passed = wf.at[model, source, c, onward[model][n]]
            shared[model, n, "on"] = start(
                copies.remote(passed, passed, copies.take(), weight_peer(step))
            )
        shared[model, n, "near"] = start(copies.remote(held, held, copies.take(), sibling))

    def forward_opposite(model, n):
        source = (y + 2) % size
        shared[model, n, "on"].wait_recv()
        held = wf.at[model, source, c, onward[model][n]]
        shared[model, n, "far"] = start(copies.remote(held, held, copies.take(), sibling))

    token_forward = {}

    def forward_tokens(model):
        at = x
        first, to_sibling = token_in[model]
        forwards = []
        for core, n, step in ((0, 0, 1), (1, 1, -1), (1, 0, 1), (0, 1, -1)):
            source = (at - step + size) % size
            arrival(nf.at[model, core, source], first + 2 * core + n).wait_recv()
            if core == n:
                forwards.append(
                    start(
                        copies.remote(
                            nf.at[model, core, source],
                            nf.at[model, core, source],
                            first + 5 + n,
                            token_peer(step, c),
                        )
                    )
                )
        token_forward[model] = (to_sibling, forwards)

    forward_weights(1, 1)
    gate(1)
    send_tokens(1)
    gate(0)
    forward_weights(1, 3)
    send_weights(0, (1, 3))
    forward_tokens(1)
    send_tokens(0)
    sums_first = copies.take(16)
    sums_local = pltpu.make_async_copy(ss_ref, sums.at[head], local.at[2])
    sums_sent = []
    for i in range(16):
        copy = pltpu.make_async_remote_copy(
            src_ref=ss_ref,
            dst_ref=sums.at[head],
            send_sem=send.at[sums_first + i],
            recv_sem=recv.at[sums_first + head],
            device_id={"seq": (seq + i) % 16, "head": seq},
            device_id_type=MESH,
        )
        sums_sent.append(copy)
        if i == 0:
            pl.when(head != seq)(copy.start)
            pl.when(head == seq)(sums_local.start)
        else:
            copy.start()

    forward_weights(1, 0)
    send_weights(0, (0, 2))
    forward_weights(1, 2)
    forward_opposite(1, 1)

    def piece(model, z_to, e):
        return part.at[model, (2 * (z_to % 2) + e - y + 4) % 4, z_to // 2]

    ring_first, ring_sends = RING_AT, RING_AT
    sent_ring = {}
    thin = rows // 4

    def ring_step(model, k, late, own=None):
        e = y % 2 if late else 1 - y % 2
        moves = []
        for v in (0, 1):
            for u, step in ((0, 1), (1, -1)):
                strip = pl.ds((2 * u + v) * thin, thin)
                z_to = (z - step * (1 + k) + 2 * ZS) % ZS
                term = piece(model, z_to, e).at[strip]
                previous, src = None, term
                if k > 0:
                    previous = sent_ring[model, late, u, v, k - 1]
                    src = ring.at[model, late, k - 1, strip]
                copy = copies.remote(
                    src,
                    ring.at[model, late, k, strip],
                    ring_first + 56 * model + 28 * late + 14 * u + 7 * v + k,
                    device(x, y, (z + step + ZS) % ZS, c),
                    ring_sends + 2 * model + late,
                )
                moves.append((previous, src, term, copy))
                sent_ring[model, late, u, v, k] = copy

        def move():
            for previous, src, term, copy in moves:
                if previous is not None:
                    previous.wait_recv()
                    src[...] = (
                        src[...].astype(jnp.float32) + term[...].astype(jnp.float32)
                    ).astype(src.dtype)
                copy.start()

        if own is None:
            move()
        elif own:
            pl.when((z + 1 + k) % 2 == y // 2)(move)
        else:
            pl.when((z + 1 + k) % 2 != y // 2)(move)

    def multiply(model, j, t):
        total = None
        for core in (0, 1):
            tokens = nf[model, core].reshape(4 * rows, nf.shape[4])
            term = jnp.dot(tokens, wf[model, j, core], preferred_element_type=jnp.float32)
            total = term if total is None else total + term
        part[model, t] = total.reshape(4, rows, total.shape[1]).astype(part.dtype)

    fin_first = copies.take(16)
    finals = []

    def finish(model, late, u):
        e = y % 2 if late else 1 - y % 2
        for v in (0, 1):
            sent_ring[model, late, u, v, 6].wait_recv()
        strip = pl.ds(2 * u * thin, 2 * thin)
        fin_src[model, late, strip] = (
            ring[model, late, 6, strip].astype(jnp.float32)
            + piece(model, z, e)[strip].astype(jnp.float32)
        ).astype(fin_src.dtype)
        src = fin_src.at[model, late, strip]
        dst = fin.at[model, c, strip]
        copy = pltpu.make_async_remote_copy(
            src_ref=src,
            dst_ref=dst,
            send_sem=send.at[fin_first + 8 * model + 2 * late + u],
            recv_sem=recv.at[fin_first + 8 * model + 2 * c + u],
            device_id=device(x, 2 * (z % 2) + e, 2 * (z // 2) + y // 2, y % 2),
            device_id_type=MESH,
        )
        if late:
            here = pltpu.make_async_copy(src, dst, local.at[5 + 2 * model + u])
            pl.when(jnp.logical_not(stays))(copy.start)
            pl.when(stays)(here.start)
            finals.append(copy)
        else:
            start(copy)

    def tokens_ready(model):
        to_sibling, forwards = token_forward[model]
        token_own[model].wait()
        to_sibling.wait_recv()
        for copy in forwards:
            copy.wait_recv()

    def product(model, t):
        at = y
        if t == 0:
            own_local[model].wait()
            forward_later[model].wait_recv()
        elif t == 1:
            shared[model, 1, "near"].wait_recv()
            shared[model, 3, "near"].wait_recv()
        elif t == 3:
            shared[model, 0, "near"].wait_recv()
            shared[model, 2, "near"].wait_recv()
        else:
            for n in onward[model]:
                shared[model, n, "far"].wait_recv()
        multiply(model, (at + t) % 4, t)

    tokens_ready(1)
    product(1, 0)
    ring_step(1, 0, 1, True)
    product(1, 1)
    product(1, 3)
    ring_step(1, 0, 0)
    ring_step(1, 1, 1, True)
    forward_opposite(1, 3)
    forward_opposite(1, 0)
    ring_step(1, 1, 0)
    ring_step(1, 2, 1, True)
    product(1, 2)
    ring_step(1, 0, 1, False)
    ring_step(1, 2, 0)
    ring_step(1, 3, 1, True)
    ring_step(1, 1, 1, False)
    forward_tokens(0)
    ring_step(1, 3, 0)
    ring_step(1, 4, 1, True)
    ring_step(1, 2, 1, False)
    forward_weights(0, 0)
    ring_step(1, 4, 0)
    ring_step(1, 5, 1, True)
    ring_step(1, 3, 1, False)
    forward_weights(0, 1)
    ring_step(1, 5, 0)
    ring_step(1, 6, 1, True)
    ring_step(1, 4, 1, False)
    forward_weights(0, 2)
    tokens_ready(0)
    product(0, 0)
    ring_step(0, 0, 1, True)
    ring_step(1, 6, 0)
    ring_step(1, 5, 1, False)
    forward_weights(0, 3)
    for u in (0, 1):
        finish(1, 0, u)
    product(0, 3)
    ring_step(0, 1, 1, True)
    product(0, 1)
    ring_step(0, 0, 0)
    ring_step(1, 6, 1, False)
    ring_step(0, 2, 1, True)
    forward_opposite(0, 0)
    for u in (0, 1):
        finish(1, 1, u)
    ring_step(0, 1, 0)
    forward_opposite(0, 1)
    ring_step(0, 2, 0)
    product(0, 2)
    ring_step(0, 0, 1, False)
    ring_step(0, 3, 1, True)
    ring_step(0, 1, 1, False)
    for k in range(3, 7):
        ring_step(0, k, 0)
        ring_step(0, k - 1, 1, False)
        if k < 6:
            ring_step(0, k + 1, 1, True)
    for u in (0, 1):
        finish(0, 0, u)
    ring_step(0, 6, 1, False)

    for i in range(16):
        here = jnp.logical_and(seq == head, head == i)
        arrived = pltpu.make_async_remote_copy(
            src_ref=ss_ref,
            dst_ref=sums.at[i],
            send_sem=send.at[sums_first + i],
            recv_sem=recv.at[sums_first + i],
            device_id=sibling,
            device_id_type=MESH,
        )
        pl.when(here)(sums_local.wait)
        pl.when(jnp.logical_not(here))(arrived.wait_recv)
    mean_square = jnp.sum(sums[...], axis=0) / 16384.0
    scale = lax.rsqrt(mean_square + 1e-05)
    columns = jnp.concatenate([scale] * 16, axis=0).T

    for u in (0, 1):
        finish(0, 1, u)
    for model in (1, 0):
        for core in (0, 1):
            from_self = jnp.logical_and(stays, c == core)
            for u in (0, 1):
                strip = pl.ds(2 * u * thin, 2 * thin)
                dst = fin.at[model, core, strip]
                landed = copies.remote(
                    dst, dst, fin_first + 8 * model + 2 * core + u, sibling
                )
                kept_here = pltpu.make_async_copy(
                    fin_src.at[model, 1, strip], dst, local.at[5 + 2 * model + u]
                )
                pl.when(jnp.logical_not(from_self))(landed.wait_recv)
                pl.when(from_self)(kept_here.wait)
            out_ref[model, core * rows : (core + 1) * rows] = (
                fin[model, core].astype(jnp.float32)
                * columns[:, 2 * model + core : 2 * model + core + 1]
            ).astype(out_ref.dtype)

    for copy in started:
        copy.wait_send()
    for model in (0, 1):
        for late in (0, 1):
            whole = ring.at[model, late]
            copies.remote(
                whole, whole, ring_first, sibling, ring_sends + 2 * model + late
            ).wait_send()
    assert copies.used <= RING_AT
    for i, copy in enumerate(sums_sent):
        if i == 0:
            pl.when(head != seq)(copy.wait_send)
        else:
            copy.wait_send()
    for copy in finals:
        pl.when(jnp.logical_not(stays))(copy.wait_send)


def local(
    x_heads, gate_z, b_proj, c_proj, dt_raw, dt_bias, decay_rate, skip_d, norm_gain, w_out, seg_ids
):
    tokens, lanes = x_heads.shape[1], x_heads.shape[2]
    depth, width = w_out.shape[1], w_out.shape[2]
    state, rows = b_proj.shape[2], tokens // 2
    bf16, f32 = jnp.bfloat16, jnp.float32
    vmem = pl.BlockSpec(memory_space=pltpu.VMEM)
    hbm = pl.BlockSpec(memory_space=pl.ANY)
    return pl.pallas_call(
        layer_kernel,
        out_shape=jax.ShapeDtypeStruct((2, tokens, width), bf16),
        in_specs=[hbm, hbm] + [vmem] * 8 + [hbm],
        out_specs=vmem,
        scratch_shapes=[
            pltpu.VMEM((2, tokens, lanes), bf16),
            pltpu.VMEM((2, tokens, lanes), bf16),
            pltpu.VMEM((2, tokens, lanes), bf16),
            pltpu.VMEM((8, 128), f32),
            pltpu.VMEM((2, tokens, lanes), f32),
            pltpu.VMEM((tokens, tokens), f32),
            pltpu.VMEM((tokens, tokens), f32),
            pltpu.VMEM((dt_raw.shape[2], lanes), bf16),
            pltpu.VMEM((8, tokens), f32),
            pltpu.VMEM((3, 8, tokens), f32),
            pltpu.VMEM((2, state, lanes), f32),
            pltpu.VMEM((2, state, lanes), bf16),
            pltpu.VMEM((2, state, lanes), bf16),
            pltpu.VMEM((2, state, lanes), bf16),
            pltpu.VMEM((2, 2, state, lanes), bf16),
            pltpu.VMEM((8, lanes), f32),
            pltpu.VMEM((8, lanes), f32),
            pltpu.VMEM((2, 4, 2, depth, width), bf16),
            pltpu.VMEM((2, 2, 4, rows, depth), bf16),
            pltpu.VMEM((2, 4, 4, rows, width), bf16),
            pltpu.VMEM((2, 2, 7, rows, width), bf16),
            pltpu.VMEM((2, 2, rows, width), bf16),
            pltpu.VMEM((2, 2, rows, width), bf16),
            pltpu.VMEM((16, 8, 128), f32),
            pltpu.SemaphoreType.DMA((RING_AT + 4,)),
            pltpu.SemaphoreType.DMA((RING_AT + 112,)),
            pltpu.SemaphoreType.DMA((11,)),
        ],
        compiler_params=pltpu.CompilerParams(
            collective_id=0, has_side_effects=True, vmem_limit_bytes=62 * 1024 * 1024
        ),
    )(
        x_heads,
        gate_z,
        b_proj,
        c_proj,
        jnp.transpose(dt_raw, (0, 2, 1)),
        dt_bias,
        decay_rate,
        skip_d,
        norm_gain,
        seg_ids.reshape(1, tokens),
        w_out,
    )


def solution(mesh):
    placed = (
        P(None, "seq", "head"),
        P(None, "seq", "head"),
        P(None, "seq", None),
        P(None, "seq", None),
        P(None, "seq", "head"),
        P(None, "head"),
        P(None, "head"),
        P(None, "head"),
        P(None, "head"),
        P(None, "head", "seq"),
        P("seq"),
    )
    return jax.shard_map(
        local, mesh=mesh, in_specs=placed, out_specs=P(None, "head", "seq"), check_vma=False
    )
```

```python
import functools

import jax
import jax.numpy as jnp
from jax import lax
from jax.experimental import pallas as pl
from jax.experimental.pallas import tpu as pltpu
from jax.sharding import PartitionSpec as P

highest = lax.Precision.HIGHEST
FAR = -1e30
RING_AT = 85

MESH = pl.DeviceIdType.MESH
XS, YS, ZS = 4, 4, 8


class Copies:
    def __init__(self, send, recv):
        self.send, self.recv, self.used, self.sends = send, recv, 0, 0

    def take(self, count=1, sends=None):
        first = self.used
        self.used += count
        self.sends += count if sends is None else sends
        return first

    def remote(self, src, dst, slot, device, send_slot=None):
        return pltpu.make_async_remote_copy(
            src_ref=src,
            dst_ref=dst,
            send_sem=self.send.at[slot if send_slot is None else send_slot],
            recv_sem=self.recv.at[slot],
            device_id=device,
            device_id_type=MESH,
        )


def layer_kernel(
    x_hbm, g_hbm, b_ref, c_ref, dt_ref, bias_ref, rate_ref, skip_ref, gain_ref, seg_ref, w_ref,
    out_ref,
    xv, gv, n_ref, ss_ref, inner, mask, products, spread, seg_own, seg_before,
    local_state, state_out, state_in, pair_out, pair_in, decay_own, decay_two,
    wf, nf, part, ring, fin_src, fin, sums, send, recv, local,
):
    seq, head = lax.axis_index("seq"), lax.axis_index("head")
    x, y = seq // YS, seq % YS
    z, c = head // 2, head % 2
    other = 1 - c

    def device(x_at, y_at, z_at, c_at):
        return {"seq": x_at * YS + y_at, "head": z_at * 2 + c_at}

    copies = Copies(send, recv)
    started = []

    def start(copy):
        copy.start()
        started.append(copy)
        return copy

    sibling = device(x, y, z, other)

    def weight_peer(step):
        return device(x, (y + step) % YS, z, c)

    def token_peer(step, core):
        return device((x + step) % XS, y, z, core)

    half = wf.shape[3] // 2
    rows = nf.shape[3]
    tokens, lanes = xv.shape[1], xv.shape[2]
    heads = dt_ref.shape[1]
    upper, lower = pl.ds(0, half), pl.ds(half, half)

    x_copy = pltpu.make_async_copy(x_hbm, xv, local.at[9])
    g_copy = pltpu.make_async_copy(g_hbm, gv, local.at[10])
    x_copy.start()

    def follower(distance):
        return {"seq": (seq + distance) % 16, "head": head}

    barrier = pltpu.get_barrier_semaphore()

    def greet(target):
        pl.semaphore_signal(barrier, inc=1, device_id=target, device_id_type=MESH)

    greet(sibling)
    for step in (1, -1):
        for core in (0, 1):
            greet(device((x + step + XS) % XS, y, z, core))
            greet(device(x, (y + step + YS) % YS, z, core))
        greet(device(x, y, (z + step + ZS) % ZS, c))
    for distance in (1, 2, 3):
        greet(follower(16 - distance))
    stays = jnp.logical_and(z % 2 == y // 2, c == y % 2)
    for core in (0, 1):
        pl.when(jnp.logical_not(jnp.logical_and(stays, c == core)))(
            functools.partial(
                greet, device(x, 2 * (z % 2) + c, 2 * (z // 2) + y // 2, core)
            )
        )
    for i in range(16):
        pl.when(jnp.logical_not(jnp.logical_and(seq == head, head == i)))(
            functools.partial(greet, {"seq": head, "head": i})
        )
    greeted = 32 - stays.astype(jnp.int32) - (seq == head).astype(jnp.int32)

    seg_row = seg_ref[...].astype(jnp.float32)
    seg_own[...] = jnp.broadcast_to(seg_row, seg_own.shape)

    arrived = {}
    size = YS
    own_local = []
    weight_slot = [copies.take(5) for model in (0, 1)]
    order = ((1, upper, 0), (-1, lower, 1), (1, lower, 2), (-1, upper, 3))

    def send_weights(model, which):
        at = y
        for step, part_rows, n in order:
            if n in which:
                copy = start(
                    copies.remote(
                        w_ref.at[model, part_rows],
                        wf.at[model, at, c, part_rows],
                        weight_slot[model] + n,
                        weight_peer(step),
                    )
                )
                arrived[model, n] = copy

    g_copy.start()
    forward_later = {}
    for model in (0, 1):
        at = y
        own = pltpu.make_async_copy(w_ref.at[model], wf.at[model, at, c], local.at[model])
        own.start()
        own_local.append(own)

    def share_own(model):
        forward_later[model] = start(
            copies.remote(
                w_ref.at[model],
                wf.at[model, y, c],
                weight_slot[model] + 4,
                sibling,
            )
        )

    row_at = lax.broadcasted_iota(jnp.int32, (tokens, tokens), 0)
    col_at = lax.broadcasted_iota(jnp.int32, (tokens, tokens), 1)
    eye = (row_at == col_at).astype(jnp.float32)
    lower_ones = (row_at >= col_at).astype(jnp.float32)
    seg_col = lax.dot_general(
        eye, seg_own[...], (((1,), (1,)), ((), ())), precision=highest
    )[:, 0:1]
    mask[...] = jnp.where(
        jnp.logical_and(row_at >= col_at, jnp.abs(seg_col - seg_row) < 0.5), 0.0, FAR
    )
    spread[...] = (
        lax.broadcasted_iota(jnp.int32, spread.shape, 0)
        == lax.broadcasted_iota(jnp.int32, spread.shape, 1) // (lanes // heads)
    ).astype(spread.dtype)
    same_last = (jnp.abs(seg_col - seg_row[:, tokens - 1 : tokens]) < 0.5).astype(jnp.float32)

    def widen(values, columns):
        coarse = values.astype(jnp.bfloat16)
        fine = (values - coarse.astype(jnp.float32)).astype(jnp.bfloat16)
        table = spread[:, columns]
        return jnp.dot(coarse, table, preferred_element_type=jnp.float32) + jnp.dot(
            fine, table, preferred_element_type=jnp.float32
        )

    blocks = [pl.ds(start_at, 256) for start_at in range(0, lanes, 256)]
    state_first = copies.take(2)
    state_copies, running, shifted, totals, tails = {}, {}, {}, {}, {}
    for model in (1, 0):
        raw = (
            lax.dot_general(eye, dt_ref[model], (((1,), (1,)), ((), ())), precision=highest)
            + bias_ref[model : model + 1, :]
        )
        step_size = jnp.maximum(raw, 0.0) + jnp.log1p(jnp.exp(-jnp.abs(raw)))
        log_decay = -(rate_ref[model : model + 1, :] * step_size)
        run = jnp.dot(lower_ones, log_decay, precision=highest)
        total = run[tokens - 1 : tokens, :]
        tails[model] = jnp.exp(total - run) * same_last * step_size
        running[model] = run
        totals[model] = total
        shifted[model] = run - jnp.log(step_size)
        seg_own[1 + model : 2 + model, 0:heads] = total

    def own_state(model):
        for block in blocks:
            weighted = (
                xv[model, :, block].astype(jnp.float32) * widen(tails[model], block)
            ).astype(jnp.bfloat16)
            fresh = lax.dot_general(
                b_ref[model],
                weighted,
                (((0,), (0,)), ((), ())),
                preferred_element_type=jnp.float32,
            )
            local_state[model, :, block] = fresh
            state_out[model, :, block] = fresh.astype(jnp.bfloat16)

    def send_state(model):
        state_copies[model] = start(
            copies.remote(
                state_out.at[model], state_in.at[model], state_first + model, follower(1)
            )
        )

    x_copy.wait()
    own_state(1)
    pl.semaphore_wait(barrier, greeted)
    info_first = copies.take(3)
    info_copies = [
        start(copies.remote(seg_own, seg_before.at[i], info_first + i, follower(i + 1)))
        for i in range(3)
    ]
    send_state(1)
    send_weights(1, (1,))
    own_state(0)
    send_state(0)
    share_own(1)
    share_own(0)

    for copy in info_copies:
        copy.wait_recv()

    def last_of(block_at):
        if block_at == 0:
            return seg_row[:, tokens - 1 : tokens]
        return seg_before[block_at - 1, 0:1, tokens - 1 : tokens]

    def decay_over(block_at, model, total):
        present = jnp.where(seq > block_at, 1.0, 0.0)
        same = (jnp.abs(last_of(block_at) - last_of(block_at + 1)) < 0.5).astype(jnp.float32)
        return jnp.exp(total) * same * present

    entered = (jnp.abs(seg_col - last_of(1)) < 0.5).astype(jnp.float32) * jnp.where(
        seq > 0, 1.0, 0.0
    )
    for model in (1, 0):
        near_decay = decay_over(0, model, totals[model])
        two = decay_over(1, model, seg_before[0, 1 + model : 2 + model, 0:heads]) * decay_over(
            2, model, seg_before[1, 1 + model : 2 + model, 0:heads]
        )
        for block in blocks:
            decay_own[model : model + 1, block] = widen(
                jnp.broadcast_to(near_decay, (8, heads)), block
            )[0:1, :]
            decay_two[model : model + 1, block] = widen(
                jnp.broadcast_to(two, (8, heads)), block
            )[0:1, :]

    def inside(model):
        run = running[model]
        shifted_t = lax.dot_general(
            shifted[model], eye, (((0,), (0,)), ((), ())), precision=highest
        )
        products[...] = lax.dot_general(
            c_ref[model],
            b_ref[model],
            (((1,), (1,)), ((), ())),
            preferred_element_type=jnp.float32,
        )
        lane = lax.broadcasted_iota(jnp.int32, (1, 128), 1)
        skip = jnp.broadcast_to(skip_ref[model : model + 1, :], (8, heads))
        mid = tokens // 2
        for pair in range(heads // 2):
            columns = pl.ds(128 * pair, 128)
            x_pair = xv[model, :, columns]
            early = late = None
            for q in (0, 1):
                h = 2 * pair + q
                x_one = x_pair * (lane // 64 == q).astype(jnp.bfloat16)
                gap = run[:mid, h : h + 1] - shifted_t[h : h + 1, :mid] + mask[:mid, :mid]
                weights = (jnp.exp(gap) * products[:mid, :mid]).astype(jnp.bfloat16)
                term = jnp.dot(weights, x_one[:mid], preferred_element_type=jnp.float32)
                early = term if early is None else early + term
                gap = run[mid:, h : h + 1] - shifted_t[h : h + 1, :] + mask[mid:, :]
                weights = (jnp.exp(gap) * products[mid:, :]).astype(jnp.bfloat16)
                term = jnp.dot(weights, x_one, preferred_element_type=jnp.float32)
                late = term if late is None else late + term
            passed = x_pair.astype(jnp.float32) * widen(skip, columns)[0:1, :]
            inner[model, :mid, columns] = early + passed[:mid]
            inner[model, mid:, columns] = late + passed[mid:]

    pair_first = copies.take(4)
    pair_copies = {}

    def join_pair(model):
        state_copies[model].wait_recv()
        for block in blocks:
            pair_out[model, :, block] = (
                local_state[model, :, block]
                + decay_own[model : model + 1, block] * state_in[model, :, block].astype(jnp.float32)
            ).astype(jnp.bfloat16)
        pair_copies[model] = [
            start(
                copies.remote(
                    pair_out.at[model],
                    pair_in.at[model, i],
                    pair_first + 2 * model + i,
                    follower(1 + 2 * i),
                )
            )
            for i in (1, 0)
        ]

    def gate(model):
        entry_w = jnp.exp(running[model]) * entered
        squares = jnp.zeros((tokens, 128), jnp.float32)
        for copy in pair_copies[model]:
            copy.wait_recv()
        for block in blocks:
            earlier = pair_in[model, 0, :, block].astype(jnp.float32) + decay_two[
                model : model + 1, block
            ] * pair_in[model, 1, :, block].astype(jnp.float32)
            entering = jnp.dot(
                c_ref[model], earlier.astype(jnp.bfloat16), preferred_element_type=jnp.float32
            )
            ssd_out = inner[model, :, block] + widen(entry_w, block) * entering
            opened = gv[model, :, block].astype(jnp.float32)
            gated = ssd_out * (opened / (1.0 + jnp.exp(-opened)))
            squares = squares + (
                gated[:, :128] * gated[:, :128] + gated[:, 128:] * gated[:, 128:]
            )
            n_ref[model, :, block] = (gated * gain_ref[model : model + 1, block]).astype(
                jnp.bfloat16
            )
        sums_row = lax.dot_general(
            jnp.ones((8, 128), jnp.float32),
            squares,
            (((1,), (1,)), ((), ())),
            precision=highest,
        )
        ss_ref[2 * model : 2 * model + 1, :] = sums_row[0:1, :128]
        ss_ref[2 * model + 1 : 2 * model + 2, :] = sums_row[0:1, 128:]

    inside(1)
    join_pair(1)
    inside(0)
    join_pair(0)
    send_weights(1, (3, 0, 2))
    g_copy.wait()
    ss_ref[...] = jnp.zeros_like(ss_ref)

    token_in = {}
    token_own = {}

    def send_tokens(model):
        at = x
        mine = pl.ds(pl.multiple_of(c * rows, rows), rows)
        theirs = pl.ds(pl.multiple_of(other * rows, rows), rows)
        own = pltpu.make_async_copy(n_ref.at[model, mine], nf.at[model, c, at], local.at[3 + model])
        own.start()
        token_own[model] = own
        first = copies.take(8)
        to_sibling = start(
            copies.remote(n_ref.at[model, theirs], nf.at[model, c, at], first + 4, sibling)
        )
        sends = []
        for core in (0, 1):
            for n, step in ((0, 1), (1, -1)):
                piece = n_ref.at[model, pl.ds(core * rows, rows)]
                copy = pltpu.make_async_remote_copy(
                    src_ref=piece,
                    dst_ref=nf.at[model, c, at],
                    send_sem=send.at[first + 2 * core + n],
                    recv_sem=recv.at[first + 2 * c + n],
                    device_id=token_peer(step, core),
                    device_id_type=MESH,
                )
                sends.append(start(copy))
        token_in[model] = (first, to_sibling)

    def arrival(dst, slot):
        return copies.remote(dst, dst, slot, sibling)

    shared = {}
    onward = {
        1: {1: lower, 3: pl.ds(half // 2, half // 2), 0: pl.ds(0, half // 2)},
        0: {0: upper, 1: lower},
    }

    def forward_weights(model, n):
        at = y
        step, part_rows = order[n][0], order[n][1]
        source = (at - step + size) % size
        arrived[model, n].wait_recv()
        held = wf.at[model, source, c, part_rows]
        if n in onward[model]:
            passed = wf.at[model, source, c, onward[model][n]]
            shared[model, n, "on"] = start(
                copies.remote(passed, passed, copies.take(), weight_peer(step))
            )
        shared[model, n, "near"] = start(copies.remote(held, held, copies.take(), sibling))

    def forward_opposite(model, n):
        source = (y + 2) % size
        shared[model, n, "on"].wait_recv()
        held = wf.at[model, source, c, onward[model][n]]
        shared[model, n, "far"] = start(copies.remote(held, held, copies.take(), sibling))

    token_forward = {}

    def forward_tokens(model):
        at = x
        first, to_sibling = token_in[model]
        forwards = []
        for core, n, step in ((0, 0, 1), (1, 1, -1), (1, 0, 1), (0, 1, -1)):
            source = (at - step + size) % size
            arrival(nf.at[model, core, source], first + 2 * core + n).wait_recv()
            if core == n:
                forwards.append(
                    start(
                        copies.remote(
                            nf.at[model, core, source],
                            nf.at[model, core, source],
                            first + 5 + n,
                            token_peer(step, c),
                        )
                    )
                )
        token_forward[model] = (to_sibling, forwards)

    forward_weights(1, 1)
    gate(1)
    send_tokens(1)
    gate(0)
    forward_weights(1, 3)
    send_weights(0, (1, 3))
    forward_tokens(1)
    send_tokens(0)
    sums_first = copies.take(16)
    sums_local = pltpu.make_async_copy(ss_ref, sums.at[head], local.at[2])
    sums_sent = []
    for i in range(16):
        copy = pltpu.make_async_remote_copy(
            src_ref=ss_ref,
            dst_ref=sums.at[head],
            send_sem=send.at[sums_first + i],
            recv_sem=recv.at[sums_first + head],
            device_id={"seq": (seq + i) % 16, "head": seq},
            device_id_type=MESH,
        )
        sums_sent.append(copy)
        if i == 0:
            pl.when(head != seq)(copy.start)
            pl.when(head == seq)(sums_local.start)
        else:
            copy.start()

    forward_weights(1, 0)
    send_weights(0, (0, 2))
    forward_weights(1, 2)
    forward_opposite(1, 1)

    def piece(model, z_to, e):
        return part.at[model, (2 * (z_to % 2) + e - y + 4) % 4, z_to // 2]

    ring_first, ring_sends = RING_AT, RING_AT
    sent_ring = {}
    thin = rows // 4

    def ring_step(model, k, late, own=None):
        e = y % 2 if late else 1 - y % 2
        moves = []
        for v in (0, 1):
            for u, step in ((0, 1), (1, -1)):
                strip = pl.ds((2 * u + v) * thin, thin)
                z_to = (z - step * (1 + k) + 2 * ZS) % ZS
                term = piece(model, z_to, e).at[strip]
                previous, src = None, term
                if k > 0:
                    previous = sent_ring[model, late, u, v, k - 1]
                    src = ring.at[model, late, k - 1, strip]
                copy = copies.remote(
                    src,
                    ring.at[model, late, k, strip],
                    ring_first + 56 * model + 28 * late + 14 * u + 7 * v + k,
                    device(x, y, (z + step + ZS) % ZS, c),
                    ring_sends + 2 * model + late,
                )
                moves.append((previous, src, term, copy))
                sent_ring[model, late, u, v, k] = copy

        def move():
            for previous, src, term, copy in moves:
                if previous is not None:
                    previous.wait_recv()
                    src[...] = (
                        src[...].astype(jnp.float32) + term[...].astype(jnp.float32)
                    ).astype(src.dtype)
                copy.start()

        if own is None:
            move()
        elif own:
            pl.when((z + 1 + k) % 2 == y // 2)(move)
        else:
            pl.when((z + 1 + k) % 2 != y // 2)(move)

    def multiply(model, j, t):
        total = None
        for core in (0, 1):
            tokens = nf[model, core].reshape(4 * rows, nf.shape[4])
            term = jnp.dot(tokens, wf[model, j, core], preferred_element_type=jnp.float32)
            total = term if total is None else total + term
        part[model, t] = total.reshape(4, rows, total.shape[1]).astype(part.dtype)

    fin_first = copies.take(16)
    finals = []

    def finish(model, late, u):
        e = y % 2 if late else 1 - y % 2
        for v in (0, 1):
            sent_ring[model, late, u, v, 6].wait_recv()
        strip = pl.ds(2 * u * thin, 2 * thin)
        fin_src[model, late, strip] = (
            ring[model, late, 6, strip].astype(jnp.float32)
            + piece(model, z, e)[strip].astype(jnp.float32)
        ).astype(fin_src.dtype)
        src = fin_src.at[model, late, strip]
        dst = fin.at[model, c, strip]
        copy = pltpu.make_async_remote_copy(
            src_ref=src,
            dst_ref=dst,
            send_sem=send.at[fin_first + 8 * model + 2 * late + u],
            recv_sem=recv.at[fin_first + 8 * model + 2 * c + u],
            device_id=device(x, 2 * (z % 2) + e, 2 * (z // 2) + y // 2, y % 2),
            device_id_type=MESH,
        )
        if late:
            here = pltpu.make_async_copy(src, dst, local.at[5 + 2 * model + u])
            pl.when(jnp.logical_not(stays))(copy.start)
            pl.when(stays)(here.start)
            finals.append(copy)
        else:
            start(copy)

    def tokens_ready(model):
        to_sibling, forwards = token_forward[model]
        token_own[model].wait()
        to_sibling.wait_recv()
        for copy in forwards:
            copy.wait_recv()

    def product(model, t):
        at = y
        if t == 0:
            own_local[model].wait()
            forward_later[model].wait_recv()
        elif t == 1:
            shared[model, 1, "near"].wait_recv()
            shared[model, 3, "near"].wait_recv()
        elif t == 3:
            shared[model, 0, "near"].wait_recv()
            shared[model, 2, "near"].wait_recv()
        else:
            for n in onward[model]:
                shared[model, n, "far"].wait_recv()
        multiply(model, (at + t) % 4, t)

    tokens_ready(1)
    product(1, 0)
    ring_step(1, 0, 1, True)
    product(1, 1)
    product(1, 3)
    ring_step(1, 0, 0)
    ring_step(1, 1, 1, True)
    forward_opposite(1, 3)
    forward_opposite(1, 0)
    ring_step(1, 1, 0)
    ring_step(1, 2, 1, True)
    product(1, 2)
    ring_step(1, 0, 1, False)
    ring_step(1, 2, 0)
    ring_step(1, 3, 1, True)
    ring_step(1, 1, 1, False)
    forward_tokens(0)
    ring_step(1, 3, 0)
    ring_step(1, 4, 1, True)
    ring_step(1, 2, 1, False)
    forward_weights(0, 0)
    ring_step(1, 4, 0)
    ring_step(1, 5, 1, True)
    ring_step(1, 3, 1, False)
    forward_weights(0, 1)
    ring_step(1, 5, 0)
    ring_step(1, 6, 1, True)
    ring_step(1, 4, 1, False)
    forward_weights(0, 2)
    tokens_ready(0)
    product(0, 0)
    ring_step(0, 0, 1, True)
    ring_step(1, 6, 0)
    ring_step(1, 5, 1, False)
    forward_weights(0, 3)
    product(0, 3)
    ring_step(0, 1, 1, True)
    product(0, 1)
    ring_step(0, 0, 0)
    ring_step(1, 6, 1, False)
    forward_opposite(0, 0)
    ring_step(0, 2, 1, True)
    ring_step(0, 1, 0)
    for u in (0, 1):
        finish(1, 0, u)
    forward_opposite(0, 1)
    ring_step(0, 2, 0)
    product(0, 2)
    ring_step(0, 0, 1, False)
    ring_step(0, 3, 1, True)
    ring_step(0, 1, 1, False)
    for u in (0, 1):
        finish(1, 1, u)
    for k in range(3, 7):
        ring_step(0, k, 0)
        ring_step(0, k - 1, 1, False)
        if k < 6:
            ring_step(0, k + 1, 1, True)
    for u in (0, 1):
        finish(0, 0, u)
    ring_step(0, 6, 1, False)

    for i in range(16):
        here = jnp.logical_and(seq == head, head == i)
        arrived = pltpu.make_async_remote_copy(
            src_ref=ss_ref,
            dst_ref=sums.at[i],
            send_sem=send.at[sums_first + i],
            recv_sem=recv.at[sums_first + i],
            device_id=sibling,
            device_id_type=MESH,
        )
        pl.when(here)(sums_local.wait)
        pl.when(jnp.logical_not(here))(arrived.wait_recv)
    mean_square = jnp.sum(sums[...], axis=0) / 16384.0
    scale = lax.rsqrt(mean_square + 1e-05)
    columns = jnp.concatenate([scale] * 16, axis=0).T

    for u in (0, 1):
        finish(0, 1, u)
    for model in (1, 0):
        for core in (0, 1):
            from_self = jnp.logical_and(stays, c == core)
            for u in (0, 1):
                strip = pl.ds(2 * u * thin, 2 * thin)
                dst = fin.at[model, core, strip]
                landed = copies.remote(
                    dst, dst, fin_first + 8 * model + 2 * core + u, sibling
                )
                kept_here = pltpu.make_async_copy(
                    fin_src.at[model, 1, strip], dst, local.at[5 + 2 * model + u]
                )
                pl.when(jnp.logical_not(from_self))(landed.wait_recv)
                pl.when(from_self)(kept_here.wait)
            out_ref[model, core * rows : (core + 1) * rows] = (
                fin[model, core].astype(jnp.float32)
                * columns[:, 2 * model + core : 2 * model + core + 1]
            ).astype(out_ref.dtype)

    for copy in started:
        copy.wait_send()
    for model in (0, 1):
        for late in (0, 1):
            whole = ring.at[model, late]
            copies.remote(
                whole, whole, ring_first, sibling, ring_sends + 2 * model + late
            ).wait_send()
    assert copies.used <= RING_AT
    for i, copy in enumerate(sums_sent):
        if i == 0:
            pl.when(head != seq)(copy.wait_send)
        else:
            copy.wait_send()
    for copy in finals:
        pl.when(jnp.logical_not(stays))(copy.wait_send)


def local(
    x_heads, gate_z, b_proj, c_proj, dt_raw, dt_bias, decay_rate, skip_d, norm_gain, w_out, seg_ids
):
    tokens, lanes = x_heads.shape[1], x_heads.shape[2]
    depth, width = w_out.shape[1], w_out.shape[2]
    state, rows = b_proj.shape[2], tokens // 2
    bf16, f32 = jnp.bfloat16, jnp.float32
    vmem = pl.BlockSpec(memory_space=pltpu.VMEM)
    hbm = pl.BlockSpec(memory_space=pl.ANY)
    return pl.pallas_call(
        layer_kernel,
        out_shape=jax.ShapeDtypeStruct((2, tokens, width), bf16),
        in_specs=[hbm, hbm] + [vmem] * 8 + [hbm],
        out_specs=vmem,
        scratch_shapes=[
            pltpu.VMEM((2, tokens, lanes), bf16),
            pltpu.VMEM((2, tokens, lanes), bf16),
            pltpu.VMEM((2, tokens, lanes), bf16),
            pltpu.VMEM((8, 128), f32),
            pltpu.VMEM((2, tokens, lanes), f32),
            pltpu.VMEM((tokens, tokens), f32),
            pltpu.VMEM((tokens, tokens), f32),
            pltpu.VMEM((dt_raw.shape[2], lanes), bf16),
            pltpu.VMEM((8, tokens), f32),
            pltpu.VMEM((3, 8, tokens), f32),
            pltpu.VMEM((2, state, lanes), f32),
            pltpu.VMEM((2, state, lanes), bf16),
            pltpu.VMEM((2, state, lanes), bf16),
            pltpu.VMEM((2, state, lanes), bf16),
            pltpu.VMEM((2, 2, state, lanes), bf16),
            pltpu.VMEM((8, lanes), f32),
            pltpu.VMEM((8, lanes), f32),
            pltpu.VMEM((2, 4, 2, depth, width), bf16),
            pltpu.VMEM((2, 2, 4, rows, depth), bf16),
            pltpu.VMEM((2, 4, 4, rows, width), bf16),
            pltpu.VMEM((2, 2, 7, rows, width), bf16),
            pltpu.VMEM((2, 2, rows, width), bf16),
            pltpu.VMEM((2, 2, rows, width), bf16),
            pltpu.VMEM((16, 8, 128), f32),
            pltpu.SemaphoreType.DMA((RING_AT + 4,)),
            pltpu.SemaphoreType.DMA((RING_AT + 112,)),
            pltpu.SemaphoreType.DMA((11,)),
        ],
        compiler_params=pltpu.CompilerParams(
            collective_id=0, has_side_effects=True, vmem_limit_bytes=62 * 1024 * 1024
        ),
    )(
        x_heads,
        gate_z,
        b_proj,
        c_proj,
        jnp.transpose(dt_raw, (0, 2, 1)),
        dt_bias,
        decay_rate,
        skip_d,
        norm_gain,
        seg_ids.reshape(1, tokens),
        w_out,
    )


def solution(mesh):
    placed = (
        P(None, "seq", "head"),
        P(None, "seq", "head"),
        P(None, "seq", None),
        P(None, "seq", None),
        P(None, "seq", "head"),
        P(None, "head"),
        P(None, "head"),
        P(None, "head"),
        P(None, "head"),
        P(None, "head", "seq"),
        P("seq"),
    )
    return jax.shard_map(
        local, mesh=mesh, in_specs=placed, out_specs=P(None, "head", "seq"), check_vma=False
    )
```
